32 devices in a mesh: seq: 2 (over x), fsdp: 16 (over z, y, core).
Axes of the slice: x: 2, y: 2, z: 4, core: 2. Of those that a mesh axis runs over, the one named last changes fastest.
Arguments:
- tokens: bfloat16 [2, 16, 1024, 768], P(None, 'fsdp', 'seq'), may hold values from -6 to 6
- doc_ids: int32 [2, 16, 1024], P(None, 'fsdp', 'seq'), may hold values from 0 to 5, never falling along the last dimension, each value on 1 to 512 neighbouring positions
- cotangent: bfloat16 [2, 16, 1024, 768], P(None, 'fsdp', 'seq'), may hold values from -6 to 6
- w_query: bfloat16 [768, 768], P('fsdp'), may hold values from -0.3125 to 0.3125
- w_key: bfloat16 [768, 768], P('fsdp'), may hold values from -0.3125 to 0.3125
- w_value: bfloat16 [768, 768], P('fsdp'), may hold values from -0.21875 to 0.21875
- w_out: bfloat16 [768, 768], P('fsdp'), may hold values from -0.875 to 0.875
- w_gate: bfloat16 [768, 2048], P('fsdp'), may hold values from -0.21875 to 0.21875
- w_up: bfloat16 [768, 2048], P('fsdp'), may hold values from -0.21875 to 0.21875
- w_down: bfloat16 [2048, 768], P('fsdp'), may hold values from -0.125 to 0.125
- gain_attn: bfloat16 [768], P('fsdp'), may hold values from 0.5 to 1.5
- gain_ffn: bfloat16 [768], P('fsdp'), may hold values from 0.5 to 1.5
Outputs:
- output: bfloat16 [2, 16, 1024, 768], P(None, 'fsdp', 'seq')
- grad_tokens: float32 [2, 16, 1024, 768], P(None, 'fsdp', 'seq')
- grad_w_query: float32 [768, 768], P('fsdp')
- grad_w_key: float32 [768, 768], P('fsdp')
- grad_w_value: float32 [768, 768], P('fsdp')
- grad_w_out: float32 [768, 768], P('fsdp')
- grad_w_gate: float32 [768, 2048], P('fsdp')
- grad_w_up: float32 [768, 2048], P('fsdp')
- grad_w_down: float32 [2048, 768], P('fsdp')
- grad_gain_attn: float32 [768], P('fsdp')
- grad_gain_ffn: float32 [768], P('fsdp')
The draws below stay inside these ranges and needn't reach their ends.
Inputs may be any that keep to these rules, and one draw needn't show every extreme that they name: Along each sequence doc_ids starts at 0 and never falls; each of the 6 documents holds 1 to 512 positions and one holds exactly 512.
All inputs are finite; a program needn't handle non-finite values.
Results may differ from the reference program's by a relative error of at most 0.017.
The reference program's roundings to bfloat16 on the way count: a program that leaves them out, or rounds other values in their place, can miss the bound.
Values may be sent and summed in bfloat16 or wider, within the bound.
No kernel may reach another device: no remote copies, remote signals or barrier semaphores. Data moves between devices by JAX's collectives and lax.ppermute only.
A program may use at most 192 MiB of HBM per device.

```python
import math
import jax
import jax.numpy as jnp
import numpy as np
from jax import lax

D = 768
HEADS = 12
HEAD_DIM = 64
FF = 2048
MICRO = 2
DOCS = 6
BATCH = 16
LEN = 1024
MOST = 512


def with_spikes(values, own_key, source, target, shards_of, factor):
    owner, partner = [(jnp.arange(values.shape[axis_at]) // (values.shape[axis_at] // shards_of)).reshape([-1 if axis == axis_at else 1 for axis in range(values.ndim)]) for axis_at in (source, target)]
    chosen = jax.random.permutation(own_key, shards_of)[partner]
    strong = (owner == chosen) | (owner == (partner + shards_of // 2) % shards_of)
    return jnp.where(strong, factor * values, values)


def levels(key, shape, split, smallest, top_value):
    level, own = 1.0, jax.random.fold_in(key, 6)
    for dim, blocks in split:
        heights = jnp.exp(jax.random.uniform(jax.random.fold_in(own, dim), (blocks,), jnp.float32, smallest / len(split), top_value / len(split)))
        level = level * jnp.repeat(heights, shape[dim] // blocks).reshape([-1 if axis == dim else 1 for axis in range(len(shape))])
    return level


def length_profile(count, total, limit, lean):
    portions = [(1 << 20) // math.isqrt(rank ** lean) + 1 for rank in range(2, count + 1)]
    spare, counts = total - limit - (count - 1), [1] * (count - 1)
    while spare > 0:
        movable = [i for i in range(count - 1) if counts[i] < limit]
        mass, budget = sum([portions[i] for i in movable]), spare
        for i in movable:
            more = min(limit - counts[i], max(1, budget * portions[i] // mass), spare)
            counts[i] = counts[i] + more
            spare = spare - more
    return np.array([limit] + counts)


def uneven_parts(own_key, amount, total, most, slope):
    if amount == 2:
        one = jax.random.randint(own_key, (), max(1, total - most), min(most, total - 1) + 1)
        return jnp.stack([one, total - one])
    lengths = jnp.asarray(length_profile(amount, total, most, slope), jnp.int32)
    twos = (amount - 1) // 2
    giver, taker = lengths[1:1 + 2 * twos:2], lengths[2:2 + 2 * twos:2]
    room = jnp.minimum(giver - 1, most - taker)
    passed = jax.random.randint(jax.random.fold_in(own_key, 1), (twos,), 0, 1 << 20) % (room + 1)
    lengths = lengths.at[1:1 + 2 * twos:2].set(giver - passed).at[2:2 + 2 * twos:2].set(taker + passed)
    return lengths[jax.random.permutation(jax.random.fold_in(own_key, 2), amount)]


def centred(own_key, dims, scale, reach, pieces=(), held_as=jnp.bfloat16):
    array = scale * jax.random.normal(own_key, dims, jnp.float32)
    if pieces:
        array = array * levels(own_key, dims, pieces, -0.22, 0.18)
    return jnp.clip(array, -reach, reach).astype(held_as)


def gaussian_with(key, dims, width, bound, shards, heavy, kind=jnp.bfloat16):
    entries = width * jax.random.normal(key, dims, jnp.float32)
    if shards:
        entries = entries * levels(key, dims, shards, -0.22, 0.18)
    return jnp.clip(with_spikes(entries, jax.random.fold_in(key, 3), *heavy), -bound, bound).astype(kind)


def setup_inputs(seed: int = 0) -> dict:
    key_of = jax.random.split(jax.random.key(seed), 13)
    tokens = gaussian_with(key_of[0], (MICRO, BATCH, LEN, D), 1.0, 6.0, ((1, 16), (2, 2)), (1, 3, 16, 2.0))
    doc_ids = jax.vmap(lambda own: jnp.searchsorted(jnp.cumsum(uneven_parts(own, DOCS, LEN, MOST, 2)), jnp.arange(LEN), side="right"))(jax.random.split(key_of[1], MICRO * BATCH)).reshape((MICRO, BATCH, LEN)).astype(jnp.int32)
    cotangent = gaussian_with(key_of[2], (MICRO, BATCH, LEN, D), 1.0, 6.0, ((1, 16), (2, 2)), (1, 3, 16, 2.0))
    w_query = centred(key_of[3], (D, D), (D // 2) ** -0.5, 0.3125, ((0, 16),))
    w_key = centred(key_of[4], (D, D), (D // 2) ** -0.5, 0.3125, ((0, 16),))
    w_value = centred(key_of[5], (D, D), D ** -0.5, 0.21875, ((0, 16),))
    w_out = centred(key_of[6], (D, D), (D // 16) ** -0.5, 0.875, ((0, 16),))
    w_gate = centred(key_of[7], (D, FF), D ** -0.5, 0.21875, ((0, 16),))
    w_up = centred(key_of[8], (D, FF), D ** -0.5, 0.21875, ((0, 16),))
    w_down = centred(key_of[9], (FF, D), FF ** -0.5, 0.125, ((0, 16),))
    gain_attn = jnp.clip(1.0 + 0.1 * jax.random.normal(key_of[10], (D,), jnp.float32), 0.5, 1.5).astype(jnp.bfloat16)
    gain_ffn = jnp.clip(1.0 + 0.1 * jax.random.normal(key_of[11], (D,), jnp.float32), 0.5, 1.5).astype(jnp.bfloat16)
    return {"tokens": tokens, "doc_ids": doc_ids, "cotangent": cotangent, "w_query": w_query, "w_key": w_key, "w_value": w_value, "w_out": w_out, "w_gate": w_gate, "w_up": w_up, "w_down": w_down, "gain_attn": gain_attn, "gain_ffn": gain_ffn}


@jax.custom_vjp
def low(v):
    return lax.optimization_barrier(v.astype(jnp.bfloat16)).astype(jnp.float32)

@jax.custom_vjp
def low_back(v):
    return v

def low_keep(v):
    return (low(v), None)

def low_pass(kept, grad):
    return (grad,)

def back_keep(v):
    return (v, None)

def back_low(kept, grad):
    return (low(grad),)
low.defvjp(low_keep, low_pass)
low_back.defvjp(back_keep, back_low)
EPSILON = 1e-05
MASK_FILL = -1e+30
HIGHEST_PREC = lax.Precision.HIGHEST

def rope_tables(positions, head_dim):
    half_dim = head_dim // 2
    inverse = jnp.exp(jnp.arange(half_dim, dtype=jnp.float32) * (-2.0 * math.log(10000.0) / head_dim))
    angles = positions[:, None] * inverse[None, :]
    return (jnp.cos(angles)[:, None, :], jnp.sin(angles)[:, None, :])

def rotate(values, cosine, sine_part):
    half_dim = values.shape[-1] // 2
    first_half = values[..., :half_dim]
    second_half = values[..., half_dim:]
    return jnp.concatenate([first_half * cosine - second_half * sine_part, second_half * cosine + first_half * sine_part], axis=-1)

def matmul(left, right):
    return jnp.dot(left, right, precision=HIGHEST_PREC)

def block_layer(params, inputs, doc_row):
    w_query, w_key, w_value, w_out, w_gate, w_up, w_down, gain_attn, gain_ffn = params
    length = inputs.shape[0]
    inv_first = lax.rsqrt(lax.optimization_barrier(jnp.mean(inputs * inputs, axis=-1, keepdims=True)) + EPSILON)
    normed = low(inputs * inv_first * gain_attn)
    cosine, sine_part = rope_tables(jnp.arange(length).astype(jnp.float32), HEAD_DIM)

    def rotated(weight):
        linear = low_back(matmul(normed, weight)).reshape(length, HEADS, HEAD_DIM)
        return low_back(low(rotate(linear, cosine, sine_part)))
    queries = rotated(w_query)
    key_rot = rotated(w_key)
    values = low_back(low(matmul(normed, w_value))).reshape(length, HEADS, HEAD_DIM)
    scores = low_back(low(jnp.einsum('qhd,khd->hqk', queries, key_rot, precision=HIGHEST_PREC) * HEAD_DIM ** (-0.5)))
    positions_all = jnp.arange(length)
    allowed = (doc_row[:, None] == doc_row[None, :]) & (positions_all[:, None] >= positions_all[None, :])
    scores = jnp.where(allowed[None, :, :], scores, MASK_FILL)
    row_max = lax.optimization_barrier(jnp.max(scores, axis=-1, keepdims=True))
    log_total = row_max + jnp.log(lax.optimization_barrier(jnp.sum(jnp.exp(scores - row_max), axis=-1, keepdims=True)))
    prob_soft = low(jnp.exp(scores - log_total))
    attended = jnp.einsum('hqk,khd->qhd', prob_soft, values, precision=HIGHEST_PREC)
    attended = low_back(low(attended.reshape(length, HEADS * HEAD_DIM)))
    middle = inputs + low_back(matmul(attended, w_out))
    inv_second = lax.rsqrt(lax.optimization_barrier(jnp.mean(middle * middle, axis=-1, keepdims=True)) + EPSILON)
    normed_two = low(middle * inv_second * gain_ffn)
    gate_proj = low_back(matmul(normed_two, w_gate))
    up_proj = low_back(matmul(normed_two, w_up))
    hidden = low(jax.nn.silu(gate_proj) * up_proj)
    return middle + matmul(hidden, w_down)

def reference(tokens, doc_ids, cotangent, w_query, w_key, w_value, w_out, w_gate, w_up, w_down, gain_attn, gain_ffn):
    params = tuple((weight.astype(jnp.float32) for weight in (w_query, w_key, w_value, w_out, w_gate, w_up, w_down, gain_attn, gain_ffn)))
    count_seqs = MICRO * BATCH
    inputs = tokens.astype(jnp.float32).reshape(count_seqs, LEN, D)
    doc_rows = doc_ids.reshape(count_seqs, LEN)
    grads_out = cotangent.astype(jnp.float32).reshape(count_seqs, LEN, D)

    def seq_step(totals, seq_item):
        seq_inputs, seq_docs, seq_grad = seq_item

        def apply_layer(weights_all, values):
            return block_layer(weights_all, values, seq_docs)
        result, pullback = jax.vjp(apply_layer, params, seq_inputs)
        grad_params, grad_inputs = pullback(seq_grad)
        totals = jax.tree.map(jnp.add, totals, grad_params)
        return (totals, (result, grad_inputs))
    zeros_all = jax.tree.map(jnp.zeros_like, params)
    totals, (results, grad_inputs) = lax.scan(seq_step, zeros_all, (inputs, doc_rows, grads_out))
    output = results.reshape(tokens.shape).astype(jnp.bfloat16)
    grad_tokens = grad_inputs.reshape(tokens.shape)
    return (output, grad_tokens, totals[0], totals[1], totals[2], totals[3], totals[4], totals[5], totals[6], totals[7], totals[8])
```

```python
import functools
import math

import jax
import jax.numpy as jnp
from jax import lax
from jax.experimental import pallas as pl
from jax.experimental.pallas import tpu as pltpu
from jax.sharding import PartitionSpec as P

HEAD_DIM = 64
EPSILON = 1e-05
MASK_FILL = -1e30
LONGEST = 512
PAIR = 2 * HEAD_DIM
QBLOCK = 128
TBLOCK = 256
BF = jnp.bfloat16
F32 = jnp.float32
ANY = pl.BlockSpec(memory_space=pl.ANY)


def cost(flops, nbytes, trans=0):
    return pl.CostEstimate(flops=int(flops), bytes_accessed=int(nbytes), transcendentals=int(trans))


def whole(shape):
    zeros = (0,) * len(shape)
    return pl.BlockSpec(shape, lambda *_: zeros)


def dot_nt(left, right):
    return lax.dot_general(left, right, (((1,), (1,)), ((), ())), preferred_element_type=F32)


def dot_nn(left, right):
    return lax.dot_general(left, right, (((1,), (0,)), ((), ())), preferred_element_type=F32)


def swap_halves(values):
    lane = lax.broadcasted_iota(jnp.int32, values.shape, 1)
    width = values.shape[1]
    half = HEAD_DIM // 2
    ahead = pltpu.roll(values, width - half, 1)
    behind = pltpu.roll(values, half, 1)
    return jnp.where((lane & (HEAD_DIM - 1)) < half, ahead, behind)


def wide(table, width):
    return jnp.concatenate([table] * (width // table.shape[1]), axis=1)


def load_copies(pieces, scratch, sems):
    rows = pieces[0].shape[0]
    me = lax.axis_index("fsdp")
    copies = []
    for place, piece in enumerate(pieces):
        if len(pieces) == 1:
            target = scratch
        else:
            owner = lax.bitwise_xor(me, place)
            target = scratch.at[pl.ds(pl.multiple_of(owner * rows, 16), rows), :]
        copies.append(pltpu.make_async_copy(piece, target, sems.at[place]))
    return copies


def rows_of(block):
    return jnp.transpose(block.astype(F32))[0:8, :]


def project_kernel(count, width, *refs):
    x_ref, cos_ref, sin_ref = refs[:3]
    pieces = refs[3 : 3 + count]
    n_ref, q_ref, k_ref, v_ref, gains_ref = refs[3 + count : 8 + count]
    weights, gain, sems = refs[8 + count :]

    @pl.when(pl.program_id(0) == 0)
    def _():
        copies = load_copies(pieces, weights, sems)
        for copy in copies:
            copy.start()
        for copy in copies:
            copy.wait()
        gain[...] = rows_of(weights[:, 3 * width : 3 * width + 128])
        gains_ref[...] = gain[...]

    x = x_ref[...].astype(F32)
    inverse = lax.rsqrt(jnp.mean(x * x, axis=1, keepdims=True) + EPSILON)
    normed = (x * inverse * gain[0:1, :]).astype(BF)
    n_ref[...] = normed
    cosine, sine = cos_ref[...], sin_ref[...]
    for part, out in enumerate((q_ref, k_ref)):
        for at in range(0, width, 256):
            linear = dot_nn(normed, weights[:, part * width + at : part * width + at + 256])
            turned = linear * wide(cosine, 256) + swap_halves(linear) * wide(sine, 256)
            turned = turned.astype(BF)
            if part == 0:
                turned = turned * jnp.asarray(HEAD_DIM**-0.5, BF)
            out[:, at : at + 256] = turned
    v_ref[...] = dot_nn(normed, weights[:, 2 * width : 3 * width]).astype(BF)


def project(x, cosine, sine, pieces):
    tokens, width = x.shape
    total = pieces[0].shape[1]
    shape = jax.ShapeDtypeStruct((tokens, width), BF)
    block = pl.BlockSpec((TBLOCK, width), lambda i: (i, 0))
    table = pl.BlockSpec((TBLOCK, PAIR), lambda i: (i, 0))
    return pl.pallas_call(
        functools.partial(project_kernel, len(pieces), width),
        name="project",
        out_shape=[shape] * 4 + [jax.ShapeDtypeStruct((8, width), F32)],
        grid=(tokens // TBLOCK,),
        in_specs=[block, table, table] + [ANY] * len(pieces),
        out_specs=[block] * 4 + [whole((8, width))],
        scratch_shapes=[
            pltpu.VMEM((width, total), BF),
            pltpu.VMEM((8, width), F32),
            pltpu.SemaphoreType.DMA((len(pieces),)),
        ],
        cost_estimate=cost(6 * tokens * width * width, 6 * width * width + 10 * tokens * width),
    )(x, cosine, sine, *pieces)


def split_heads(values):
    lane = lax.broadcasted_iota(jnp.int32, values.shape, 1)
    zero = jnp.zeros_like(values)
    return jnp.concatenate(
        [jnp.where(lane < HEAD_DIM, values, zero), jnp.where(lane < HEAD_DIM, zero, values)], axis=0
    )


def join_heads(both):
    rows = both.shape[1] // 2
    own = jnp.concatenate([both[:HEAD_DIM, :rows], both[HEAD_DIM:, rows:]], axis=0)
    return jnp.transpose(own)


def masked_bias(starts_row, first_key, span, first_row):
    key = first_key + lax.broadcasted_iota(jnp.int32, (span, QBLOCK), 0)
    query = first_row + lax.broadcasted_iota(jnp.int32, (span, QBLOCK), 1)
    allowed = (key >= starts_row) & (key <= query)
    return jnp.where(allowed, 0.0, MASK_FILL)


def per_span(first_ref, length, body):
    block = pl.program_id(0)
    seen = block - first_ref[block] + 1
    most = min(length, LONGEST + QBLOCK) // QBLOCK
    for blocks in range(1, most + 1):

        @pl.when(seen == blocks)
        def _(blocks=blocks):
            first_key = pl.multiple_of((block - blocks + 1) * QBLOCK, QBLOCK)
            body(blocks * QBLOCK, first_key, block * QBLOCK)


def attend_kernel(pairs, first_ref, q_ref, k_ref, v_ref, starts_ref, out_ref, lse_ref, v_turned, bias):
    @pl.when(pl.program_id(0) == 0)
    def _():
        v_turned[...] = jnp.transpose(v_ref[...])

    def body(span, first_key, first_row):
        bias[:span, :] = masked_bias(starts_ref[...], first_key, span, first_row)
        for pair in range(pairs):
            lanes = slice(pair * PAIR, (pair + 1) * PAIR)
            queries = split_heads(q_ref[:, lanes])
            scores = dot_nt(k_ref[pl.ds(first_key, span), lanes], queries)
            fill = bias[:span, :]
            scores = scores.astype(BF).astype(F32) + jnp.concatenate([fill, fill], axis=1)
            top = jnp.max(scores, axis=0, keepdims=True)
            weights = jnp.exp(scores - top)
            total = jnp.sum(weights, axis=0, keepdims=True)
            lse_ref[0, pair : pair + 1, :] = top + jnp.log(total)
            weights = (weights * (1.0 / total)).astype(BF)
            both = dot_nn(v_turned[lanes, pl.ds(first_key, span)], weights)
            out_ref[:, lanes] = join_heads(both).astype(BF)

    per_span(first_ref, k_ref.shape[0], body)


def attend(queries, keys, values, starts, first):
    length, width = queries.shape
    pairs = width // PAIR
    blocks = length // QBLOCK
    block = pl.BlockSpec((QBLOCK, width), lambda i, f: (i, 0))
    return pl.pallas_call(
        functools.partial(attend_kernel, pairs),
        name="attend",
        out_shape=[
            jax.ShapeDtypeStruct((length, width), BF),
            jax.ShapeDtypeStruct((blocks, pairs, 2 * QBLOCK), F32),
        ],
        grid_spec=pltpu.PrefetchScalarGridSpec(
            num_scalar_prefetch=1,
            grid=(blocks,),
            in_specs=[
                block,
                whole((length, width)),
                whole((length, width)),
                pl.BlockSpec((1, QBLOCK), lambda i, f: (0, i)),
            ],
            out_specs=[block, pl.BlockSpec((1, pairs, 2 * QBLOCK), lambda i, f: (i, 0, 0))],
            scratch_shapes=[
                pltpu.VMEM((width, length), BF),
                pltpu.VMEM((min(length, LONGEST + QBLOCK), QBLOCK), F32),
            ],
        ),
        cost_estimate=cost(4 * length * length * width, 10 * length * width),
    )(first, queries, keys, values, starts)


def attend_back_kernel(
    pairs, first_ref, q_ref, k_ref, v_ref, g_ref, lse_ref, starts_ref, cos_ref, sin_ref, out_ref, k_turned, bias, dk, dv
):
    width = pairs * PAIR
    block = pl.program_id(0)

    @pl.when(block == 0)
    def _():
        k_turned[...] = jnp.transpose(k_ref[...])
        dk[...] = jnp.zeros_like(dk)
        dv[...] = jnp.zeros_like(dv)

    rows = pl.ds(pl.multiple_of(block * QBLOCK, QBLOCK), QBLOCK)
    cosine, sine = cos_ref[rows, :], sin_ref[rows, :]

    def body(span, first_key, first_row):
        bias[:span, :] = masked_bias(starts_ref[...], first_key, span, first_row)
        keys_at = pl.ds(first_key, span)
        for pair in range(pairs):
            lanes = slice(pair * PAIR, (pair + 1) * PAIR)
            queries = split_heads(q_ref[:, lanes])
            grads = split_heads(g_ref[:, lanes])
            scores = dot_nt(k_ref[keys_at, lanes], queries)
            grad_probs = dot_nt(v_ref[keys_at, lanes], grads)
            fill = bias[:span, :]
            scores = scores.astype(BF).astype(F32) + jnp.concatenate([fill, fill], axis=1)
            probs = jnp.exp(scores - lse_ref[0, pair : pair + 1, :])
            dv[keys_at, lanes] += dot_nn(probs.astype(BF), grads)
            delta = jnp.sum(probs * grad_probs, axis=0, keepdims=True)
            grad_scores = (probs * (grad_probs - delta)).astype(BF)
            dk[keys_at, lanes] += dot_nn(grad_scores, queries)
            both = dot_nn(k_turned[lanes, keys_at], grad_scores)
            dq = (join_heads(both) * HEAD_DIM**-0.5).astype(BF).astype(F32)
            out_ref[rows, lanes] = (dq * cosine - swap_halves(dq) * sine).astype(BF)

    per_span(first_ref, k_ref.shape[0], body)

    @pl.when(block == pl.num_programs(0) - 1)
    def _():
        def finish(step, carry):
            at = pl.ds(pl.multiple_of(step * QBLOCK, QBLOCK), QBLOCK)
            turn, slant = cos_ref[at, :], sin_ref[at, :]
            for pair in range(pairs):
                lanes = slice(pair * PAIR, (pair + 1) * PAIR)
                grad = dk[at, lanes].astype(BF).astype(F32)
                out_ref[at, width + pair * PAIR : width + (pair + 1) * PAIR] = (
                    grad * turn - swap_halves(grad) * slant
                ).astype(BF)
            out_ref[at, 2 * width : 3 * width] = dv[at, :].astype(BF)
            return carry

        lax.fori_loop(0, k_ref.shape[0] // QBLOCK, finish, 0)


def attend_back(queries, keys, values, grads, lse, starts, first, cosine, sine):
    length, width = queries.shape
    pairs = width // PAIR
    blocks = length // QBLOCK
    block = pl.BlockSpec((QBLOCK, width), lambda i, f: (i, 0))
    full = whole((length, width))
    table = whole((length, PAIR))
    return pl.pallas_call(
        functools.partial(attend_back_kernel, pairs),
        name="attend_back",
        out_shape=jax.ShapeDtypeStruct((length, 3 * width), BF),
        grid_spec=pltpu.PrefetchScalarGridSpec(
            num_scalar_prefetch=1,
            grid=(blocks,),
            in_specs=[
                block,
                full,
                full,
                block,
                pl.BlockSpec((1, pairs, 2 * QBLOCK), lambda i, f: (i, 0, 0)),
                pl.BlockSpec((1, QBLOCK), lambda i, f: (0, i)),
                table,
                table,
            ],
            out_specs=whole((length, 3 * width)),
            scratch_shapes=[
                pltpu.VMEM((width, length), BF),
                pltpu.VMEM((min(length, LONGEST + QBLOCK), QBLOCK), F32),
                pltpu.VMEM((length, width), F32),
                pltpu.VMEM((length, width), F32),
            ],
        ),
        cost_estimate=cost(10 * length * length * width, 16 * length * width),
    )(first, queries, keys, values, grads, lse, starts, cosine, sine)


def feed_kernel(counts, width, hidden_width, *refs):
    x_ref, att_ref, dy_ref, gain_ref = refs[:4]
    refs = refs[4:]
    first, refs = refs[: counts[0]], refs[counts[0] :]
    second, refs = refs[: counts[1]], refs[counts[1] :]
    y_ref, n_ref, hid_ref, dgate_ref, dup_ref, dm_ref, dmr_ref, datt_ref = refs[:8]
    w_first, w_down, sems_first, sems_second = refs[8:]

    @pl.when(pl.program_id(0) == 0)
    def _():
        copies = load_copies(first, w_first, sems_first) + load_copies(second, w_down, sems_second)
        for copy in copies:
            copy.start()
        for copy in copies:
            copy.wait()

    gain = gain_ref[1:2, :]
    dy = dy_ref[...]
    middle = x_ref[...].astype(F32) + dot_nn(att_ref[...], w_first[:, :width])
    inverse = lax.rsqrt(jnp.mean(middle * middle, axis=1, keepdims=True) + EPSILON)
    normed = (middle * inverse * gain).astype(BF)
    n_ref[...] = normed
    result = middle
    back = jnp.zeros_like(middle)
    step = min(512, hidden_width)
    for at in range(0, hidden_width, step):
        part = slice(at, at + step)
        w_gate = w_first[:, width + at : width + at + step]
        w_up = w_first[:, width + hidden_width + at : width + hidden_width + at + step]
        gate = dot_nn(normed, w_gate)
        up = dot_nn(normed, w_up)
        sigma = 1.0 / (1.0 + jnp.exp(-gate))
        silu = gate * sigma
        hidden = (silu * up).astype(BF)
        hid_ref[:, part] = hidden
        result = result + dot_nn(hidden, w_down[part, :])
        dh = dot_nt(dy, w_down[part, :])
        dgate = (dh * up * sigma * (1.0 + gate * (1.0 - sigma))).astype(BF)
        dup = (dh * silu).astype(BF)
        dgate_ref[:, part] = dgate
        dup_ref[:, part] = dup
        back = back + dot_nt(dgate, w_gate) + dot_nt(dup, w_up)
    y_ref[...] = result.astype(BF)
    scaled = back * gain
    dm = dy.astype(F32) + inverse * scaled - middle * (inverse * inverse * inverse) * jnp.mean(
        scaled * middle, axis=1, keepdims=True
    )
    dm_ref[...] = dm
    dmr = dm.astype(BF)
    dmr_ref[...] = dmr
    datt_ref[...] = dot_nt(dmr, w_first[:, :width]).astype(BF)


def feed(x, attended, dy, gain, first, second, hidden_width):
    tokens, width = x.shape
    block = pl.BlockSpec((TBLOCK, width), lambda i: (i, 0))
    broad = pl.BlockSpec((TBLOCK, hidden_width), lambda i: (i, 0))
    narrow, large = jax.ShapeDtypeStruct((tokens, width), BF), jax.ShapeDtypeStruct((tokens, hidden_width), BF)
    return pl.pallas_call(
        functools.partial(feed_kernel, (len(first), len(second)), width, hidden_width),
        name="feed",
        out_shape=[narrow, narrow, large, large, large, jax.ShapeDtypeStruct((tokens, width), F32), narrow, narrow],
        grid=(tokens // TBLOCK,),
        in_specs=[block, block, block, whole((8, width))] + [ANY] * (len(first) + len(second)),
        out_specs=[block, block, broad, broad, broad, block, block, block],
        scratch_shapes=[
            pltpu.VMEM((width, width + 2 * hidden_width), BF),
            pltpu.VMEM((hidden_width, width), BF),
            pltpu.SemaphoreType.DMA((len(first),)),
            pltpu.SemaphoreType.DMA((len(second),)),
        ],
        cost_estimate=cost(4 * tokens * width * (width + 3 * hidden_width), 20 * tokens * width + 6 * tokens * hidden_width),
    )(x, attended, dy, gain, *first, *second)


def write_pieces(parts, total, keep, send):
    if parts == 1:
        keep[...] = total[...].astype(BF)
        return
    rows = total.shape[0] // parts
    me = lax.axis_index("fsdp")
    for place in range(parts // 2):
        upper, y_bit = place % (parts // 4), place // (parts // 4)
        for core, out in enumerate((keep, send)):
            owner = lax.bitwise_xor(me, upper * 4 + y_bit * 2 + core)
            out[place] = total[pl.ds(pl.multiple_of(owner * rows, 16), rows), :].astype(BF)


def outer_kernel(parts, edges, *refs):
    count = len(edges)
    lefts, rights = refs[:count], refs[count : 2 * count]
    outs = refs[2 * count : -1 - count]
    turned, total = refs[-1 - count : -1], refs[-1]
    step = pl.program_id(0)
    low = 0
    for left, right, turn, high in zip(lefts, rights, turned, edges):

        @pl.when(step == low)
        def _(left=left, turn=turn):
            turn[...] = jnp.transpose(left[...])

        @pl.when((step >= low) & (step < high))
        def _(right=right, turn=turn):
            total[...] = dot_nn(turn[...], right[...])

        low = high
    write_pieces(parts, total, *((outs + (None,))[:2]))


def outer_sums(parts, lefts, rights, name):
    tile = 256
    tokens, rows = lefts[0].shape
    edges, specs, low = [], [], 0
    for right in rights:
        steps = right.shape[1] // tile
        specs.append(
            pl.BlockSpec((tokens, tile), lambda j, low=low, steps=steps: (0, jnp.clip(j - low, 0, steps - 1)))
        )
        low += steps
        edges.append(low)
    width = low * tile
    kept_lefts, kept_edges = [], []
    shape = (rows, width) if parts == 1 else (parts // 2, rows // parts, width)
    out_block = (rows, tile) if parts == 1 else (parts // 2, rows // parts, tile)
    index = (lambda j: (0, j)) if parts == 1 else (lambda j: (0, 0, j))
    n_out = 1 if parts == 1 else 2
    outs = pl.pallas_call(
        functools.partial(outer_kernel, parts, tuple(edges)),
        name=name,
        out_shape=[jax.ShapeDtypeStruct(shape, BF)] * n_out,
        grid=(low,),
        in_specs=[whole((tokens, rows)) for _ in lefts] + specs,
        out_specs=[pl.BlockSpec(out_block, index)] * n_out,
        scratch_shapes=[pltpu.VMEM((rows, tokens), BF) for _ in lefts] + [pltpu.VMEM((rows, tile), F32)],
        cost_estimate=cost(2 * tokens * rows * width, 2 * tokens * (rows + width) + 2 * rows * width),
    )(*lefts, *rights)
    return outs


def input_grad_kernel(count, width, *refs):
    x_ref, dm_ref, grads_ref, gains_ref = refs[:4]
    pieces = refs[4 : 4 + count]
    out_ref = refs[4 + count]
    weights, sems = refs[5 + count :]

    @pl.when(pl.program_id(0) == 0)
    def _():
        copies = load_copies(pieces, weights, sems)
        for copy in copies:
            copy.start()
        for copy in copies:
            copy.wait()

    x = x_ref[...].astype(F32)
    inverse = lax.rsqrt(jnp.mean(x * x, axis=1, keepdims=True) + EPSILON)
    scaled = dot_nt(grads_ref[...], weights[:, : 3 * width]) * gains_ref[0:1, :]
    out_ref[...] = (
        dm_ref[...]
        + inverse * scaled
        - x * (inverse * inverse * inverse) * jnp.mean(scaled * x, axis=1, keepdims=True)
    )


def input_grad(x, dm, grads, gains, pieces):
    tokens, width = x.shape
    block = pl.BlockSpec((TBLOCK, width), lambda i: (i, 0))
    return pl.pallas_call(
        functools.partial(input_grad_kernel, len(pieces), width),
        name="input_grad",
        out_shape=jax.ShapeDtypeStruct((tokens, width), F32),
        grid=(tokens // TBLOCK,),
        in_specs=[block, block, pl.BlockSpec((TBLOCK, 3 * width), lambda i: (i, 0)), whole((8, width))]
        + [ANY] * len(pieces),
        out_specs=block,
        scratch_shapes=[
            pltpu.VMEM((width, pieces[0].shape[1]), BF),
            pltpu.SemaphoreType.DMA((len(pieces),)),
        ],
        cost_estimate=cost(6 * tokens * width * width, 6 * width * width + 16 * tokens * width),
    )(x, dm, grads, gains, *pieces)


def flip(values, bits):
    count = lax.axis_size("fsdp")
    return lax.ppermute(values, "fsdp", [(i, i ^ bits) for i in range(count)])


def across(values):
    return lax.ppermute(values, "seq", [(0, 1), (1, 0)])


def aligned(rows, count):
    return rows % 16 == 0 and count >= 4 and count & (count - 1) == 0


def gather_rows(shard, parts):
    if parts == 1:
        return [lax.all_gather(shard, "fsdp", axis=0, tiled=True)]
    pieces = [None] * parts
    pieces[0] = shard
    for upper in range(4, parts, 4):
        pieces[upper] = flip(shard, upper)
    for upper in range(0, parts, 4):
        pieces[upper + 2] = flip(pieces[upper], 2)
    for even in range(0, parts, 2):
        pieces[even + 1] = flip(pieces[even], 1)
    return pieces


def scatter_rows(outs, parts):
    if parts == 1:
        total = lax.psum_scatter(outs[0], "fsdp", scatter_dimension=0, tiled=True)
    else:
        keep, send = outs
        upper = parts // 4
        got = flip(send, 1)
        ahead = (keep[upper:].astype(F32) + got[upper:].astype(F32)).astype(BF)
        ahead = flip(ahead, 2)
        parts_sum = [
            keep[j].astype(F32) + got[j].astype(F32) + ahead[j].astype(F32) for j in range(upper)
        ]
        arrived = [flip(parts_sum[j].astype(BF), 4 * j) for j in range(1, upper)]
        total = parts_sum[0]
        for piece in arrived:
            total = total + piece.astype(F32)
        total = total.astype(BF)
    return total.astype(F32) + across(total).astype(F32)


def rope_tables(length):
    half = HEAD_DIM // 2
    inverse = jnp.exp(jnp.arange(half, dtype=F32) * (-2.0 * math.log(10000.0) / HEAD_DIM))
    angles = jnp.arange(length, dtype=jnp.int32).astype(F32)[:, None] * inverse[None, :]
    cosine, sine = jnp.cos(angles), jnp.sin(angles)
    return (
        jnp.concatenate([cosine] * 4, axis=1),
        jnp.concatenate([-sine, sine, -sine, sine], axis=1),
    )


def per_device(
    tokens, doc_ids, cotangent, w_query, w_key, w_value, w_out, w_gate, w_up, w_down, gain_attn, gain_ffn
):
    seq_rank = lax.axis_index("seq")
    count = lax.axis_size("fsdp")
    micro, _, span, width = tokens.shape
    hidden_width = w_gate.shape[1]
    rows = w_query.shape[0]
    parts = count if aligned(rows, count) and aligned(w_down.shape[0], count) else 1

    def mine(array):
        own = lax.dynamic_index_in_dim(array, seq_rank, 0, keepdims=False)[0]
        other = across(lax.dynamic_index_in_dim(array, 1 - seq_rank, 0, keepdims=False)[0])
        return jnp.where(seq_rank == 0, jnp.concatenate([own, other]), jnp.concatenate([other, own]))

    def halves(array):
        own = lax.dynamic_slice_in_dim(array, seq_rank * span, span, 0)
        other = lax.dynamic_slice_in_dim(array, (1 - seq_rank) * span, span, 0)
        return own, other

    def give_back(own, other):
        first, second = jnp.where(seq_rank == 0, own, other), jnp.where(seq_rank == 0, other, own)
        return jnp.stack([first, second])[:, None]

    column = jnp.pad(jnp.stack([gain_attn, gain_ffn], axis=1), ((0, 0), (0, 126)))
    group_in = jnp.concatenate([w_query, w_key, w_value, column], axis=1)
    group_mid = jnp.concatenate([w_out, w_gate, w_up], axis=1)

    x = mine(tokens)
    docs = mine(doc_ids)
    pieces_in = gather_rows(group_in, parts)
    pieces_mid = gather_rows(group_mid, parts)
    pieces_down = gather_rows(w_down, parts)
    dy = mine(cotangent)

    length = x.shape[0]
    cosine, sine = rope_tables(length)
    starts = jnp.sum((docs[None, :] < docs[:, None]).astype(jnp.int32), axis=1)
    first = starts[::QBLOCK] // QBLOCK
    starts = starts[None, :]

    normed, queries, keys, values, gains = project(x, cosine, sine, pieces_in)
    attended, lse = attend(queries, keys, values, starts, first)
    y, normed_two, hidden, dgate, dup, dm, dmr, datt = feed(
        x, attended, dy, gains, pieces_mid, pieces_down, hidden_width
    )
    own_y, other_y = halves(y)
    output = give_back(own_y, across(other_y))
    sum_down = scatter_rows(outer_sums(parts, [hidden], [dy], "grad_down"), parts)
    sum_mid = scatter_rows(
        outer_sums(parts, [attended, normed_two, normed_two], [dmr, dgate, dup], "grad_mid"), parts
    )
    grads = attend_back(queries, keys, values, datt, lse, starts, first, cosine, sine)
    sum_in = scatter_rows(outer_sums(parts, [normed], [grads], "grad_in"), parts)
    grad_x = input_grad(x, dm, grads, gains, pieces_in)
    own_g, other_g = halves(grad_x)
    grad_tokens = give_back(own_g, across(other_g.astype(BF)).astype(F32))

    sum_out, sum_gate, sum_up = (
        sum_mid[:, :width],
        sum_mid[:, width : width + hidden_width],
        sum_mid[:, width + hidden_width :],
    )
    w_in = group_in[:, : 3 * width].astype(F32)
    grad_gain_attn = jnp.sum(w_in * sum_in, axis=1) / gain_attn.astype(F32)
    grad_gain_ffn = jnp.sum(
        group_mid[:, width:].astype(F32) * sum_mid[:, width:], axis=1
    ) / gain_ffn.astype(F32)
    return (
        output,
        grad_tokens,
        sum_in[:, :width],
        sum_in[:, width : 2 * width],
        sum_in[:, 2 * width :],
        sum_out,
        sum_gate,
        sum_up,
        sum_down,
        grad_gain_attn,
        grad_gain_ffn,
    )


def solution(mesh):
    rows = P("fsdp", None)
    acts = P(None, "fsdp", "seq", None)
    return jax.shard_map(
        per_device,
        mesh=mesh,
        in_specs=(acts, P(None, "fsdp", "seq"), acts) + (rows,) * 7 + (P("fsdp"),) * 2,
        out_specs=(acts, acts) + (rows,) * 7 + (P("fsdp"),) * 2,
        check_vma=False,
    )
```

```python
import functools
import math

import jax
import jax.numpy as jnp
from jax import lax
from jax.experimental import pallas as pl
from jax.experimental.pallas import tpu as pltpu
from jax.sharding import PartitionSpec as P

HEAD_DIM = 64
EPSILON = 1e-05
MASK_FILL = -1e30
LONGEST = 512
PAIR = 2 * HEAD_DIM
QBLOCK = 128
TBLOCK = 512
FBLOCK = 512
FSTEP = 512
TILE = 1024
BF = jnp.bfloat16
F32 = jnp.float32
ANY = pl.BlockSpec(memory_space=pl.ANY)


def cost(flops, nbytes, trans=0):
    return pl.CostEstimate(flops=int(flops), bytes_accessed=int(nbytes), transcendentals=int(trans))


def whole(shape):
    zeros = (0,) * len(shape)
    return pl.BlockSpec(shape, lambda *_: zeros)


def dot_nt(left, right):
    return lax.dot_general(left, right, (((1,), (1,)), ((), ())), preferred_element_type=F32)


def dot_nn(left, right):
    return lax.dot_general(left, right, (((1,), (0,)), ((), ())), preferred_element_type=F32)


def swap_halves(values):
    lane = lax.broadcasted_iota(jnp.int32, values.shape, 1)
    width = values.shape[1]
    half = HEAD_DIM // 2
    ahead = pltpu.roll(values, width - half, 1)
    behind = pltpu.roll(values, half, 1)
    return jnp.where((lane & (HEAD_DIM - 1)) < half, ahead, behind)


def wide(table, width):
    return jnp.concatenate([table] * (width // table.shape[1]), axis=1)


def load_copies(groups, scratch, sem):
    if len(groups) == 1:
        return [pltpu.make_async_copy(groups[0][0], scratch, sem)]
    rows = scratch.shape[0] // sum(len(places) for _, places in groups)
    me = lax.axis_index("fsdp")
    copies = []
    for piece, places in groups:
        for at, place in enumerate(places):
            target = pl.ds(pl.multiple_of(lax.bitwise_xor(me, place) * rows, 16), rows)
            copies.append(pltpu.make_async_copy(piece.at[pl.ds(at * rows, rows), :], scratch.at[target, :], sem))
    return copies


def start_all(copies):
    for copy in copies:
        copy.start()


def wait_all(copies):
    for copy in copies:
        copy.wait()


def rows_of(block):
    return jnp.transpose(block.astype(F32))[0:8, :]


def project_kernel(places, width, *refs):
    x_ref, cos_ref, sin_ref = refs[:3]
    count = len(places)
    groups = list(zip(refs[3 : 3 + count], places))
    n_ref, q_ref, k_ref, v_ref, gains_ref = refs[3 + count : 8 + count]
    weights, gain, sem = refs[8 + count :]

    @pl.when(pl.program_id(0) == 0)
    def _():
        copies = load_copies(groups, weights, sem)
        start_all(copies)
        wait_all(copies)
        gain[...] = rows_of(weights[:, 3 * width : 3 * width + 128])
        gains_ref[...] = gain[...]

    x = x_ref[...].astype(F32)
    inverse = lax.rsqrt(jnp.mean(x * x, axis=1, keepdims=True) + EPSILON)
    normed = (x * inverse * gain[0:1, :]).astype(BF)
    n_ref[...] = normed
    cosine, sine = wide(cos_ref[...], width // 2), wide(sin_ref[...], width // 2)
    for part, out in enumerate((q_ref, k_ref)):
        for at in range(0, width, width // 2):
            linear = dot_nn(normed, weights[:, part * width + at : part * width + at + width // 2])
            turned = (linear * cosine + swap_halves(linear) * sine).astype(BF)
            if part == 0:
                turned = turned * jnp.asarray(HEAD_DIM**-0.5, BF)
            out[:, at : at + width // 2] = turned
    v_ref[...] = dot_nn(normed, weights[:, 2 * width : 3 * width]).astype(BF)


def project(x, cosine, sine, groups):
    tokens, width = x.shape
    total = groups[0][0].shape[1]
    shape = jax.ShapeDtypeStruct((tokens, width), BF)
    block = pl.BlockSpec((TBLOCK, width), lambda i: (i, 0))
    table = pl.BlockSpec((TBLOCK, PAIR), lambda i: (i, 0))
    return pl.pallas_call(
        functools.partial(project_kernel, [places for _, places in groups], width),
        name="project",
        out_shape=[shape] * 4 + [jax.ShapeDtypeStruct((8, width), F32)],
        grid=(tokens // TBLOCK,),
        in_specs=[block, table, table] + [ANY] * len(groups),
        out_specs=[block] * 4 + [whole((8, width))],
        scratch_shapes=[
            pltpu.VMEM((width, total), BF),
            pltpu.VMEM((8, width), F32),
            pltpu.SemaphoreType.DMA,
        ],
        cost_estimate=cost(6 * tokens * width * width, 6 * width * width + 10 * tokens * width),
    )(x, cosine, sine, *[piece for piece, _ in groups])


def split_heads(values):
    lane = lax.broadcasted_iota(jnp.int32, values.shape, 1)
    zero = jnp.zeros_like(values)
    return jnp.concatenate(
        [jnp.where(lane < HEAD_DIM, values, zero), jnp.where(lane < HEAD_DIM, zero, values)], axis=0
    )


def join_heads(both):
    rows = both.shape[1] // 2
    own = jnp.concatenate([both[:HEAD_DIM, :rows], both[HEAD_DIM:, rows:]], axis=0)
    return jnp.transpose(own)


def masked_bias(starts_row, first_key, span, first_row):
    key = first_key + lax.broadcasted_iota(jnp.int32, (span, QBLOCK), 0)
    query = first_row + lax.broadcasted_iota(jnp.int32, (span, QBLOCK), 1)
    allowed = (key >= starts_row) & (key <= query)
    return jnp.where(allowed, 0.0, MASK_FILL)


def per_span(first_ref, length, body):
    block = pl.program_id(0)
    seen = block - first_ref[block] + 1
    most = min(length, LONGEST + QBLOCK) // QBLOCK
    for blocks in range(1, most + 1):

        @pl.when(seen == blocks)
        def _(blocks=blocks):
            first_key = pl.multiple_of((block - blocks + 1) * QBLOCK, QBLOCK)
            body(blocks * QBLOCK, first_key, block * QBLOCK)


def attend_kernel(pairs, first_ref, q_ref, k_ref, v_ref, starts_ref, out_ref, lse_ref, v_turned, bias):
    @pl.when(pl.program_id(0) == 0)
    def _():
        v_turned[...] = jnp.transpose(v_ref[...])

    def body(span, first_key, first_row):
        bias[:span, :] = masked_bias(starts_ref[...], first_key, span, first_row)
        keys_at = pl.ds(first_key, span)
        lanes = [slice(pair * PAIR, (pair + 1) * PAIR) for pair in range(pairs)]
        scored, weighed = {}, {}
        for step in range(pairs + 2):
            if step < pairs:
                scored[step] = dot_nt(k_ref[keys_at, lanes[step]], split_heads(q_ref[:, lanes[step]])).astype(BF)
            pair = step - 2
            if pair >= 0:
                weights, total = weighed.pop(pair)
                both = dot_nn(v_turned[lanes[pair], keys_at], weights) * (1.0 / total)
                out_ref[:, lanes[pair]] = join_heads(both).astype(BF)
            pair = step - 1
            if 0 <= pair < pairs:
                fill = bias[:span, :]
                scores = scored.pop(pair).astype(F32) + jnp.concatenate([fill, fill], axis=1)
                top = jnp.max(scores, axis=0, keepdims=True)
                weights = jnp.exp(scores - top)
                total = jnp.sum(weights, axis=0, keepdims=True)
                lse_ref[0, pair : pair + 1, :] = top + jnp.log(total)
                weighed[pair] = (weights.astype(BF), total)

    per_span(first_ref, k_ref.shape[0], body)


def attend(queries, keys, values, starts, first):
    length, width = queries.shape
    pairs = width // PAIR
    blocks = length // QBLOCK
    block = pl.BlockSpec((QBLOCK, width), lambda i, f: (i, 0))
    return pl.pallas_call(
        functools.partial(attend_kernel, pairs),
        name="attend",
        out_shape=[
            jax.ShapeDtypeStruct((length, width), BF),
            jax.ShapeDtypeStruct((blocks, pairs, 2 * QBLOCK), F32),
        ],
        grid_spec=pltpu.PrefetchScalarGridSpec(
            num_scalar_prefetch=1,
            grid=(blocks,),
            in_specs=[
                block,
                whole((length, width)),
                whole((length, width)),
                pl.BlockSpec((1, QBLOCK), lambda i, f: (0, i)),
            ],
            out_specs=[block, pl.BlockSpec((1, pairs, 2 * QBLOCK), lambda i, f: (i, 0, 0))],
            scratch_shapes=[
                pltpu.VMEM((width, length), BF),
                pltpu.VMEM((min(length, LONGEST + QBLOCK), QBLOCK), F32),
            ],
        ),
        cost_estimate=cost(4 * length * length * width, 10 * length * width),
    )(first, queries, keys, values, starts)


def attend_back_kernel(
    pairs, first_ref, q_ref, k_ref, v_ref, g_ref, lse_ref, starts_ref, cos_ref, sin_ref, out_ref, k_turned, bias, dk, dv
):
    width = pairs * PAIR
    block = pl.program_id(0)

    @pl.when(block == 0)
    def _():
        k_turned[...] = jnp.transpose(k_ref[...])
        dk[...] = jnp.zeros_like(dk)
        dv[...] = jnp.zeros_like(dv)

    rows = pl.ds(pl.multiple_of(block * QBLOCK, QBLOCK), QBLOCK)
    cosine, sine = cos_ref[rows, :], sin_ref[rows, :]

    def body(span, first_key, first_row):
        bias[:span, :] = masked_bias(starts_ref[...], first_key, span, first_row)
        keys_at = pl.ds(first_key, span)
        lanes = [slice(pair * PAIR, (pair + 1) * PAIR) for pair in range(pairs)]
        scored, ready = {}, {}
        for step in range(pairs + 2):
            if step < pairs:
                at = lanes[step]
                queries, grads = split_heads(q_ref[:, at]), split_heads(g_ref[:, at])
                scores = dot_nt(k_ref[keys_at, at], queries).astype(BF)
                scored[step] = (scores, dot_nt(v_ref[keys_at, at], grads), queries, grads)
            pair = step - 2
            if pair >= 0:
                at = lanes[pair]
                probs, grad_scores, queries, grads = ready.pop(pair)
                dv[keys_at, at] += dot_nn(probs, grads)
                dk[keys_at, at] += dot_nn(grad_scores, queries)
                both = dot_nn(k_turned[at, keys_at], grad_scores)
                dq = (join_heads(both) * HEAD_DIM**-0.5).astype(BF).astype(F32)
                out_ref[rows, at] = (dq * cosine - swap_halves(dq) * sine).astype(BF)
            pair = step - 1
            if 0 <= pair < pairs:
                scores, grad_probs, queries, grads = scored.pop(pair)
                fill = bias[:span, :]
                scores = scores.astype(F32) + jnp.concatenate([fill, fill], axis=1)
                probs = jnp.exp(scores - lse_ref[0, pair : pair + 1, :])
                delta = jnp.sum(probs * grad_probs, axis=0, keepdims=True)
                ready[pair] = (probs.astype(BF), (probs * (grad_probs - delta)).astype(BF), queries, grads)

    per_span(first_ref, k_ref.shape[0], body)

    @pl.when(block == pl.num_programs(0) - 1)
    def _():
        def finish(step, carry):
            at = pl.ds(pl.multiple_of(step * QBLOCK, QBLOCK), QBLOCK)
            turn, slant = cos_ref[at, :], sin_ref[at, :]
            for pair in range(pairs):
                lanes = slice(pair * PAIR, (pair + 1) * PAIR)
                grad = dk[at, lanes].astype(BF).astype(F32)
                out_ref[at, width + pair * PAIR : width + (pair + 1) * PAIR] = (
                    grad * turn - swap_halves(grad) * slant
                ).astype(BF)
            out_ref[at, 2 * width : 3 * width] = dv[at, :].astype(BF)
            return carry

        lax.fori_loop(0, k_ref.shape[0] // QBLOCK, finish, 0)


def attend_back(queries, keys, values, grads, lse, starts, first, cosine, sine):
    length, width = queries.shape
    pairs = width // PAIR
    blocks = length // QBLOCK
    block = pl.BlockSpec((QBLOCK, width), lambda i, f: (i, 0))
    full = whole((length, width))
    table = whole((length, PAIR))
    return pl.pallas_call(
        functools.partial(attend_back_kernel, pairs),
        name="attend_back",
        out_shape=jax.ShapeDtypeStruct((length, 3 * width), BF),
        grid_spec=pltpu.PrefetchScalarGridSpec(
            num_scalar_prefetch=1,
            grid=(blocks,),
            in_specs=[
                block,
                full,
                full,
                block,
                pl.BlockSpec((1, pairs, 2 * QBLOCK), lambda i, f: (i, 0, 0)),
                pl.BlockSpec((1, QBLOCK), lambda i, f: (0, i)),
                table,
                table,
            ],
            out_specs=whole((length, 3 * width)),
            scratch_shapes=[
                pltpu.VMEM((width, length), BF),
                pltpu.VMEM((min(length, LONGEST + QBLOCK), QBLOCK), F32),
                pltpu.VMEM((length, width), F32),
                pltpu.VMEM((length, width), F32),
            ],
        ),
        cost_estimate=cost(10 * length * length * width, 16 * length * width),
    )(first, queries, keys, values, grads, lse, starts, cosine, sine)


def packed_slices(rows, down_rows, width, hidden_width):
    slices = [("down", (0, down_rows), (0, width), 0, 0), ("out", (0, rows), (0, width), down_rows, 0)]
    top = down_rows + rows
    both = 2 * hidden_width
    for at in range(0, both - width + 1, width):
        slices.append(("both", (0, rows), (at, at + width), top, 0))
        top += rows
    rest = both % width
    if rest:
        few = rows * rest // width
        for place in range(width // rest):
            slices.append(("both", (place * few, (place + 1) * few), (both - rest, both), top, place * rest))
        top += few
    return slices, top


def feed_copies(packed, targets, owner, sems):
    w_out, w_both, w_down = targets
    parts = w_out.shape[0] // packed[0]
    rows, down_rows = packed[0], w_down.shape[0] // parts
    slices, height = packed_slices(rows, down_rows, w_out.shape[1], w_down.shape[0])
    kinds = {"out": (w_out, rows, 0), "both": (w_both, rows, 1), "down": (w_down, down_rows, 2)}
    copies = {"out": [], "both": [], "down": []}
    for name, (low, high), (left, right), top, column in slices:
        target, each, number = kinds[name]
        source = packed[1].at[
            pl.ds(pl.multiple_of(owner * height + top, 16), high - low), column : column + right - left
        ]
        goal = target.at[pl.ds(pl.multiple_of(owner * each + low, 16), high - low), left:right]
        copies[name].append(pltpu.make_async_copy(source, goal, sems.at[number]))
    return copies


def feed_kernel(rows, count, width, hidden_width, *refs):
    x_ref, att_ref, dy_ref, gain_ref = refs[:4]
    given, refs = refs[4 : 4 + count], refs[4 + count :]
    y_ref, n_ref, hid_ref, dgate_ref, dup_ref, dm_ref, dmr_ref, datt_ref = refs[:8]
    w_out, w_both, w_down, sems = refs[8:]
    targets = (w_out, w_both, w_down)
    parts = width // rows

    def whole_copies():
        views = (w_out, w_both.at[:, :hidden_width], w_both.at[:, hidden_width:], w_down)
        return [pltpu.make_async_copy(piece, view, sems.at[0]) for piece, view in zip(given, views)]

    def per_owner(act):
        def step(owner, carry):
            act(feed_copies((rows, given[0]), targets, owner, sems))
            return carry

        lax.fori_loop(0, parts, step, 0)

    @pl.when(pl.program_id(0) == 0)
    def _():
        if count > 1:
            copies = whole_copies()
            start_all(copies)
            wait_all(copies)
        else:
            per_owner(lambda copies: start_all(copies["out"] + copies["both"] + copies["down"]))
            per_owner(lambda copies: wait_all(copies["out"] + copies["both"] + copies["down"]))

    gain = gain_ref[1:2, :]
    dy = dy_ref[...]
    middle = x_ref[...].astype(F32) + dot_nn(att_ref[...], w_out[...])
    inverse = lax.rsqrt(jnp.mean(middle * middle, axis=1, keepdims=True) + EPSILON)
    normed = (middle * inverse * gain).astype(BF)
    n_ref[...] = normed
    result = middle
    back = jnp.zeros_like(middle)
    step = min(FSTEP, hidden_width)
    for at in range(0, hidden_width, step):
        part = slice(at, at + step)
        w_gate = w_both[:, at : at + step]
        w_up = w_both[:, hidden_width + at : hidden_width + at + step]
        gate = dot_nn(normed, w_gate)
        up = dot_nn(normed, w_up)
        dh = dot_nt(dy, w_down[part, :])
        sigma = 1.0 / (1.0 + jnp.exp(-gate))
        silu = gate * sigma
        hidden = (silu * up).astype(BF)
        hid_ref[:, part] = hidden
        dgate = (dh * up * (sigma * (1.0 + gate * (1.0 - sigma)))).astype(BF)
        dup = (dh * silu).astype(BF)
        dgate_ref[:, part] = dgate
        dup_ref[:, part] = dup
        result = result + dot_nn(hidden, w_down[part, :])
        back = back + dot_nt(dgate, w_gate) + dot_nt(dup, w_up)
    y_ref[...] = result.astype(BF)
    scaled = back * gain
    dm = dy.astype(F32) + inverse * scaled - middle * (inverse * inverse * inverse) * jnp.mean(
        scaled * middle, axis=1, keepdims=True
    )
    dm_ref[...] = dm
    dmr = dm.astype(BF)
    dmr_ref[...] = dmr
    datt_ref[...] = dot_nt(dmr, w_out[...]).astype(BF)


def feed(x, attended, dy, gain, given, rows, hidden_width):
    tokens, width = x.shape
    block = pl.BlockSpec((FBLOCK, width), lambda i: (i, 0))
    broad = pl.BlockSpec((FBLOCK, hidden_width), lambda i: (i, 0))
    narrow, large = jax.ShapeDtypeStruct((tokens, width), BF), jax.ShapeDtypeStruct((tokens, hidden_width), BF)
    return pl.pallas_call(
        functools.partial(feed_kernel, rows, len(given), width, hidden_width),
        name="feed",
        out_shape=[narrow, narrow, large, large, large, jax.ShapeDtypeStruct((tokens, width), F32), narrow, narrow],
        grid=(tokens // FBLOCK,),
        in_specs=[block, block, block, whole((8, width))] + [ANY] * len(given),
        out_specs=[block, block, broad, broad, broad, block, block, block],
        scratch_shapes=[
            pltpu.VMEM((width, width), BF),
            pltpu.VMEM((width, 2 * hidden_width), BF),
            pltpu.VMEM((hidden_width, width), BF),
            pltpu.SemaphoreType.DMA((3,)),
        ],
        cost_estimate=cost(4 * tokens * width * (width + 3 * hidden_width), 20 * tokens * width + 6 * tokens * hidden_width),
    )(x, attended, dy, gain, *given)


def dot_tn(left, right):
    return lax.dot_general(left, right, (((0,), (0,)), ((), ())), preferred_element_type=F32)


def write_pieces(parts, total, keep, send):
    if parts == 1:
        keep[...] = total[...].astype(BF)
        return
    rows = total.shape[0] // parts
    me = lax.axis_index("fsdp")
    for place in range(parts // 2):
        upper, y_bit = place % (parts // 4), place // (parts // 4)
        for core, out in enumerate((keep, send)):
            owner = lax.bitwise_xor(me, upper * 4 + y_bit * 2 + core)
            out[place] = total[pl.ds(pl.multiple_of(owner * rows, 16), rows), :].astype(BF)


def outer_kernel(parts, counts, edges, *refs):
    lefts = []
    for count in counts:
        lefts.append(refs[:count])
        refs = refs[count:]
    rights, outs, total = refs[: len(counts)], refs[len(counts) : -1], refs[-1]
    step = pl.program_id(0)
    low = 0
    for group, right, high in zip(lefts, rights, edges):

        @pl.when((step >= low) & (step < high))
        def _(group=group, right=right):
            row = 0
            for left in group:
                total[row : row + left.shape[1], :] = dot_tn(left[...], right[...])
                row += left.shape[1]

        low = high
    write_pieces(parts, total, *((outs + (None,))[:2]))


def outer_sums(parts, pairs, tile, name):
    edges, specs, low = [], [], 0
    for lefts, right in pairs:
        steps = right.shape[1] // tile
        specs.append(
            pl.BlockSpec(
                (right.shape[0], tile), lambda j, low=low, steps=steps: (0, jnp.clip(j - low, 0, steps - 1))
            )
        )
        low += steps
        edges.append(low)
    width = low * tile
    tokens = pairs[0][1].shape[0]
    rows = sum(left.shape[1] for left in pairs[0][0])
    every_left = [left for lefts, _ in pairs for left in lefts]
    shape = (rows, width) if parts == 1 else (parts // 2, rows // parts, width)
    out_block = (rows, tile) if parts == 1 else (parts // 2, rows // parts, tile)
    index = (lambda j: (0, j)) if parts == 1 else (lambda j: (0, 0, j))
    n_out = 1 if parts == 1 else 2
    return pl.pallas_call(
        functools.partial(outer_kernel, parts, tuple(len(lefts) for lefts, _ in pairs), tuple(edges)),
        name=name,
        out_shape=[jax.ShapeDtypeStruct(shape, BF)] * n_out,
        grid=(low,),
        in_specs=[whole(left.shape) for left in every_left] + specs,
        out_specs=[pl.BlockSpec(out_block, index)] * n_out,
        scratch_shapes=[pltpu.VMEM((rows, tile), F32)],
        cost_estimate=cost(2 * tokens * rows * width, 2 * tokens * (rows + width) + 2 * rows * width),
    )(*every_left, *[right for _, right in pairs])


def feed_grads_kernel(parts, steps, n_ref, dgate_ref, dup_ref, hid_any, dy_any, out_ref, hidden, dy, total, sems):
    step = pl.program_id(0)
    tile = out_ref.shape[2]
    width = n_ref.shape[1]
    copies = [pltpu.make_async_copy(hid_any, hidden, sems.at[0]), pltpu.make_async_copy(dy_any, dy, sems.at[1])]

    @pl.when(step == 0)
    def _():
        start_all(copies)

    for low, right in ((0, dgate_ref), (steps, dup_ref)):

        @pl.when((step >= low) & (step < low + steps))
        def _(right=right):
            out_ref[...] = dot_tn(n_ref[...], right[...]).astype(BF).reshape(out_ref.shape)

    @pl.when(step == 2 * steps)
    def _():
        wait_all(copies)
        each = hidden.shape[1] // 2
        for at in (0, each):
            grad = dot_tn(hidden[:, at : at + each], dy[...]).astype(BF)
            total[at * parts // hidden.shape[1] : (at + each) * parts // hidden.shape[1]] = grad.reshape(
                parts // 2, hidden.shape[1] // parts, width
            )

    for place in range(steps):

        @pl.when(step == 2 * steps + place)
        def _(place=place):
            unit = 16 * parts
            for group in range(tile // unit):
                rows = slice((place * tile // unit + group) * 16, (place * tile // unit + group + 1) * 16)
                for column in range(width // unit):
                    out_ref[:, column * 16 : (column + 1) * 16, group * unit : (group + 1) * unit] = total[
                        :, rows, column * unit : (column + 1) * unit
                    ]


def feed_grads(parts, normed, dgate, dup, hidden, dy):
    tokens, width = normed.shape
    hidden_width = hidden.shape[1]
    tile = min(TILE, hidden_width)
    steps = hidden_width // tile
    rows = width // parts
    return pl.pallas_call(
        functools.partial(feed_grads_kernel, parts, steps),
        name="feed_grads",
        out_shape=jax.ShapeDtypeStruct((parts, 3 * rows, hidden_width), BF),
        grid=(3 * steps,),
        in_specs=[
            whole((tokens, width)),
            pl.BlockSpec((tokens, tile), lambda j: (0, jnp.minimum(j, steps - 1))),
            pl.BlockSpec((tokens, tile), lambda j: (0, jnp.clip(j - steps, 0, steps - 1))),
            ANY,
            ANY,
        ],
        out_specs=pl.BlockSpec((parts, rows, tile), lambda j: (0, j // steps, j % steps)),
        scratch_shapes=[
            pltpu.VMEM((tokens, hidden_width), BF),
            pltpu.VMEM((tokens, width), BF),
            pltpu.VMEM((parts, hidden_width // parts, width), BF),
            pltpu.SemaphoreType.DMA((2,)),
        ],
        cost_estimate=cost(6 * tokens * width * hidden_width, 6 * tokens * (hidden_width + width)),
    )(normed, dgate, dup, hidden, dy)


def input_grad_kernel(places, width, *refs):
    count = len(places)
    x_ref, dm_ref, grads_ref, gains_ref = refs[:4]
    groups = list(zip(refs[4 : 4 + count], places))
    out_ref, weights, sem = refs[4 + count :]

    @pl.when(pl.program_id(0) == 0)
    def _():
        copies = load_copies(groups, weights, sem)
        start_all(copies)
        wait_all(copies)

    x = x_ref[...].astype(F32)
    inverse = lax.rsqrt(jnp.mean(x * x, axis=1, keepdims=True) + EPSILON)
    scaled = dot_nt(grads_ref[...], weights[:, : 3 * width]) * gains_ref[0:1, :]
    out_ref[...] = (
        dm_ref[...]
        + inverse * scaled
        - x * (inverse * inverse * inverse) * jnp.mean(scaled * x, axis=1, keepdims=True)
    )


def input_grad(x, dm, grads, gains, groups):
    tokens, width = x.shape
    block = pl.BlockSpec((TBLOCK, width), lambda i: (i, 0))
    return pl.pallas_call(
        functools.partial(input_grad_kernel, [places for _, places in groups], width),
        name="input_grad",
        out_shape=jax.ShapeDtypeStruct((tokens, width), F32),
        grid=(tokens // TBLOCK,),
        in_specs=[block, block, pl.BlockSpec((TBLOCK, 3 * width), lambda i: (i, 0)), whole((8, width))]
        + [ANY] * len(groups),
        out_specs=block,
        scratch_shapes=[
            pltpu.VMEM((width, groups[0][0].shape[1]), BF),
            pltpu.SemaphoreType.DMA,
        ],
        cost_estimate=cost(6 * tokens * width * width, 6 * width * width + 16 * tokens * width),
    )(x, dm, grads, gains, *[piece for piece, _ in groups])


def flip(values, bits):
    count = lax.axis_size("fsdp")
    return lax.ppermute(values, "fsdp", [(i, i ^ bits) for i in range(count)])


def across(values):
    return lax.ppermute(values, "seq", [(0, 1), (1, 0)])


def aligned(rows, down_rows, width, hidden_width, count):
    rest = 2 * hidden_width % width
    return (
        count == 16
        and rows % 16 == 0
        and down_rows % 16 == 0
        and (rest == 0 or (width % rest == 0 and rows * rest % (16 * width) == 0))
    )


def gate(values, *others):
    return lax.optimization_barrier((values,) + others)[0]


def gather_rows(shard, parts):
    if parts == 1:
        return [(lax.all_gather(shard, "fsdp", axis=0, tiled=True), (0,))]
    uppers = tuple(range(0, parts, 4))
    mine = jnp.concatenate([shard] + [flip(shard, upper) for upper in uppers[1:]])
    beside = flip(mine, 2)
    groups = [(mine, 0), (beside, 2), (flip(mine, 1), 1), (flip(beside, 1), 3)]
    return [(piece, tuple(upper + low for upper in uppers)) for piece, low in groups]


def pack(w_out, w_gate, w_up, w_down):
    rows, width = w_out.shape
    sources = {"down": w_down, "out": w_out, "both": jnp.concatenate([w_gate, w_up], axis=1)}
    slices, _ = packed_slices(rows, w_down.shape[0], width, w_gate.shape[1])
    strips, line, filled = [], [], 0
    for name, (low, high), (left, right), _, _ in slices:
        line.append(sources[name][low:high, left:right])
        filled += right - left
        if filled == width:
            strips.append(line[0] if len(line) == 1 else jnp.concatenate(line, axis=1))
            line, filled = [], 0
    return jnp.concatenate(strips)


class Scatter:
    def __init__(self, outs, parts):
        self.parts = parts
        if parts == 1:
            self.total = lax.psum_scatter(outs[0], "fsdp", scatter_dimension=0, tiled=True)
            return
        self.keep, send = outs
        self.got = flip(send, 1)

    def y_hop(self):
        if self.parts == 1:
            return []
        upper = self.parts // 4
        ahead = (self.keep[upper:].astype(F32) + self.got[upper:].astype(F32)).astype(BF)
        self.ahead = flip(ahead, 2)
        return [ahead]

    def z_hop(self):
        if self.parts == 1:
            return []
        sums = [
            self.keep[j].astype(F32) + self.got[j].astype(F32) + self.ahead[j].astype(F32)
            for j in range(self.parts // 4)
        ]
        self.own, sends = sums[0], [total.astype(BF) for total in sums[1:]]
        self.others = [flip(send, 4 * (j + 1)) for j, send in enumerate(sends)]
        return sends

    def x_hop(self):
        if self.parts > 1:
            total = self.own
            for piece in self.others:
                total = total + piece.astype(F32)
            self.total = total.astype(BF)
        self.partner = across(self.total)
        return [self.total]

    def result(self):
        return self.total.astype(F32) + self.partner.astype(F32)


def rope_tables(length):
    half = HEAD_DIM // 2
    inverse = jnp.exp(jnp.arange(half, dtype=F32) * (-2.0 * math.log(10000.0) / HEAD_DIM))
    angles = jnp.arange(length, dtype=jnp.int32).astype(F32)[:, None] * inverse[None, :]
    cosine, sine = jnp.cos(angles), jnp.sin(angles)
    return (
        jnp.concatenate([cosine] * 4, axis=1),
        jnp.concatenate([-sine, sine, -sine, sine], axis=1),
    )


def per_device(
    tokens, doc_ids, cotangent, w_query, w_key, w_value, w_out, w_gate, w_up, w_down, gain_attn, gain_ffn
):
    seq_rank = lax.axis_index("seq")
    count = lax.axis_size("fsdp")
    micro, _, span, width = tokens.shape
    hidden_width = w_gate.shape[1]
    rows = w_query.shape[0]
    parts = count if aligned(rows, w_down.shape[0], width, hidden_width, count) else 1

    if parts == 1:
        given = [lax.all_gather(weight, "fsdp", axis=0, tiled=True) for weight in (w_out, w_gate, w_up, w_down)]
    else:
        given = [lax.all_gather(pack(w_out, w_gate, w_up, w_down), "fsdp", axis=0, tiled=True)]

    def exchanged(array):
        own = lax.dynamic_index_in_dim(array, seq_rank, 0, keepdims=False)[0]
        return own, lax.dynamic_index_in_dim(array, 1 - seq_rank, 0, keepdims=False)[0]

    def ordered(own, other):
        return jnp.where(seq_rank == 0, jnp.concatenate([own, other]), jnp.concatenate([other, own]))

    def halves(array):
        own = lax.dynamic_slice_in_dim(array, seq_rank * span, span, 0)
        other = lax.dynamic_slice_in_dim(array, (1 - seq_rank) * span, span, 0)
        return own, other

    def give_back(own, other):
        first, second = jnp.where(seq_rank == 0, own, other), jnp.where(seq_rank == 0, other, own)
        return jnp.stack([first, second])[:, None]

    column = jnp.pad(jnp.stack([gain_attn, gain_ffn], axis=1), ((0, 0), (0, 126)))
    w_in = jnp.concatenate([w_query, w_key, w_value, column], axis=1)
    groups_in = gather_rows(w_in, parts)
    own_x, other_x = exchanged(tokens)
    x = ordered(own_x, across(other_x))
    own_docs, other_docs = exchanged(doc_ids)
    docs = ordered(own_docs, across(other_docs))
    own_dy, other_dy = exchanged(gate(cotangent, x))
    dy = ordered(own_dy, across(other_dy))

    length = x.shape[0]
    cosine, sine = rope_tables(length)
    starts = jnp.sum((docs[None, :] < docs[:, None]).astype(jnp.int32), axis=1)
    first = starts[::QBLOCK] // QBLOCK
    starts = starts[None, :]

    normed, queries, keys, values, gains = project(x, cosine, sine, groups_in)
    attended, lse = attend(queries, keys, values, starts, first)
    y, normed_two, hidden, dgate, dup, dm, dmr, datt = feed(
        x, attended, dy, gains, given, rows if parts > 1 else width, hidden_width
    )
    own_y, other_y = halves(y)
    output = give_back(own_y, across(other_y))

    if parts == 1:
        sum_gate, sum_up, sum_down = [
            lax.psum_scatter(outer_sums(1, [(lefts, right)], tile, name)[0], "fsdp", scatter_dimension=0, tiled=True)
            for lefts, right, tile, name in (
                ([normed_two], dgate, 512, "grad_gate"),
                ([normed_two], dup, 512, "grad_up"),
                ([hidden], dy, width // 2, "grad_down"),
            )
        ]
        sums = (sum_gate, sum_up, sum_down)
    else:
        ff = feed_grads(parts, normed_two, dgate, dup, hidden, dy)
        datt = gate(datt, ff)
        ff = lax.psum_scatter(ff.reshape(-1, hidden_width), "fsdp", scatter_dimension=0, tiled=True)
        sums = (ff,)
    grads = attend_back(queries, keys, values, datt, lse, starts, first, cosine, sine)
    scatter = Scatter(outer_sums(parts, [([normed], grads), ([attended], dmr)], width, "grad_in"), parts)
    grad_x = input_grad(x, dm, grads, gains, groups_in)
    own_g, other_g = halves(grad_x)
    scatter.y_hop()
    grad_tokens = give_back(own_g, across(other_g.astype(BF)).astype(F32))
    scatter.z_hop()
    scatter.x_hop()
    sum_in = scatter.result()
    sums = [part.astype(F32) + across(part).astype(F32) for part in sums]
    if parts == 1:
        sum_gate, sum_up, sum_down = sums
    else:
        sum_gate, sum_up, rest = sums[0][:rows], sums[0][rows : 2 * rows], sums[0][2 * rows :]
        unit = 16 * parts
        rest = rest.reshape(rows // 16, 16, hidden_width // unit, unit)
        sum_down = rest.transpose(2, 1, 0, 3).reshape(w_down.shape)

    sum_in, sum_out = sum_in[:, : 3 * width], sum_in[:, 3 * width :]
    grad_gain_attn = jnp.sum(w_in[:, : 3 * width].astype(F32) * sum_in, axis=1) / gain_attn.astype(F32)
    grad_gain_ffn = (
        jnp.sum(w_gate.astype(F32) * sum_gate, axis=1) + jnp.sum(w_up.astype(F32) * sum_up, axis=1)
    ) / gain_ffn.astype(F32)
    by_part = [sum_in[:, at * width : (at + 1) * width] for at in range(3)]
    return (output, grad_tokens, *by_part, sum_out, sum_gate, sum_up, sum_down, grad_gain_attn, grad_gain_ffn)


def solution(mesh):
    rows = P("fsdp", None)
    acts = P(None, "fsdp", "seq", None)
    return jax.shard_map(
        per_device,
        mesh=mesh,
        in_specs=(acts, P(None, "fsdp", "seq"), acts) + (rows,) * 7 + (P("fsdp"),) * 2,
        out_specs=(acts, acts) + (rows,) * 7 + (P("fsdp"),) * 2,
        check_vma=False,
    )
```

```python
import functools
import math

import jax
import jax.numpy as jnp
from jax import lax
from jax.experimental import pallas as pl
from jax.experimental.pallas import tpu as pltpu
from jax.sharding import PartitionSpec as P

HEAD_DIM = 64
EPSILON = 1e-05
MASK_FILL = -1e30
LONGEST = 512
PAIR = 2 * HEAD_DIM
QBLOCK = 128
TBLOCK = 512
FBLOCK = 512
FSTEP = 512
TILE = 1024
BF = jnp.bfloat16
F32 = jnp.float32
ANY = pl.BlockSpec(memory_space=pl.ANY)


def cost(flops, nbytes, trans=0):
    return pl.CostEstimate(flops=int(flops), bytes_accessed=int(nbytes), transcendentals=int(trans))


def whole(shape):
    zeros = (0,) * len(shape)
    return pl.BlockSpec(shape, lambda *_: zeros)


def dot_nt(left, right):
    return lax.dot_general(left, right, (((1,), (1,)), ((), ())), preferred_element_type=F32)


def dot_nn(left, right):
    return lax.dot_general(left, right, (((1,), (0,)), ((), ())), preferred_element_type=F32)


def swap_halves(values):
    lane = lax.broadcasted_iota(jnp.int32, values.shape, 1)
    width = values.shape[1]
    half = HEAD_DIM // 2
    ahead = pltpu.roll(values, width - half, 1)
    behind = pltpu.roll(values, half, 1)
    return jnp.where((lane & (HEAD_DIM - 1)) < half, ahead, behind)


def wide(table, width):
    return jnp.concatenate([table] * (width // table.shape[1]), axis=1)


def load_copies(groups, scratch, sem):
    if len(groups) == 1:
        return [pltpu.make_async_copy(groups[0][0], scratch, sem)]
    me, rank = lax.axis_index("fsdp"), lax.axis_index("seq")
    rows = 2 * scratch.shape[0] // sum(len(places) for _, places, _ in groups)
    half = scratch.shape[1] // 2
    copies = []
    for piece, places, side in groups:
        columns = pl.ds(pl.multiple_of(lax.bitwise_xor(rank, side) * half, 128), half)
        for at, place in enumerate(places):
            target = pl.ds(pl.multiple_of(lax.bitwise_xor(me, place) * rows, 16), rows)
            copies.append(
                pltpu.make_async_copy(piece.at[pl.ds(at * rows, rows), :], scratch.at[target, columns], sem)
            )
    return copies


def columns_of(groups):
    return groups[0][0].shape[1] * (1 if len(groups) == 1 else 2)


def start_all(copies):
    for copy in copies:
        copy.start()


def wait_all(copies):
    for copy in copies:
        copy.wait()


def rows_of(block):
    return jnp.transpose(block.astype(F32))[0:8, :]


def project_kernel(places, width, *refs):
    x_ref, cos_ref, sin_ref = refs[:3]
    count = len(places)
    groups = [(piece, *place) for piece, place in zip(refs[3 : 3 + count], places)]
    n_ref, q_ref, k_ref, v_ref, gains_ref = refs[3 + count : 8 + count]
    weights, gain, sem = refs[8 + count :]

    @pl.when(pl.program_id(0) == 0)
    def _():
        copies = load_copies(groups, weights, sem)
        start_all(copies)
        wait_all(copies)
        gain[...] = rows_of(weights[:, 3 * width : 3 * width + 128])
        gains_ref[...] = gain[...]

    x = x_ref[...].astype(F32)
    inverse = lax.rsqrt(jnp.mean(x * x, axis=1, keepdims=True) + EPSILON)
    normed = (x * inverse * gain[0:1, :]).astype(BF)
    n_ref[...] = normed
    cosine, sine = wide(cos_ref[...], width // 2), wide(sin_ref[...], width // 2)
    for part, out in enumerate((q_ref, k_ref)):
        for at in range(0, width, width // 2):
            linear = dot_nn(normed, weights[:, part * width + at : part * width + at + width // 2])
            turned = (linear * cosine + swap_halves(linear) * sine).astype(BF)
            if part == 0:
                turned = turned * jnp.asarray(HEAD_DIM**-0.5, BF)
            out[:, at : at + width // 2] = turned
    v_ref[...] = dot_nn(normed, weights[:, 2 * width : 3 * width]).astype(BF)


def project(x, cosine, sine, groups):
    tokens, width = x.shape
    total = columns_of(groups)
    shape = jax.ShapeDtypeStruct((tokens, width), BF)
    block = pl.BlockSpec((TBLOCK, width), lambda i: (i, 0))
    table = pl.BlockSpec((TBLOCK, PAIR), lambda i: (i, 0))
    return pl.pallas_call(
        functools.partial(project_kernel, [place for _, *place in groups], width),
        name="project",
        out_shape=[shape] * 4 + [jax.ShapeDtypeStruct((8, width), F32)],
        grid=(tokens // TBLOCK,),
        in_specs=[block, table, table] + [ANY] * len(groups),
        out_specs=[block] * 4 + [whole((8, width))],
        scratch_shapes=[
            pltpu.VMEM((width, total), BF),
            pltpu.VMEM((8, width), F32),
            pltpu.SemaphoreType.DMA,
        ],
        cost_estimate=cost(6 * tokens * width * width, 6 * width * width + 10 * tokens * width),
    )(x, cosine, sine, *[piece for piece, *_ in groups])


def split_heads(values):
    lane = lax.broadcasted_iota(jnp.int32, values.shape, 1)
    zero = jnp.zeros_like(values)
    return jnp.concatenate(
        [jnp.where(lane < HEAD_DIM, values, zero), jnp.where(lane < HEAD_DIM, zero, values)], axis=0
    )


def join_heads(both):
    rows = both.shape[1] // 2
    own = jnp.concatenate([both[:HEAD_DIM, :rows], both[HEAD_DIM:, rows:]], axis=0)
    return jnp.transpose(own)


def masked_bias(starts_row, first_key, span, first_row):
    key = first_key + lax.broadcasted_iota(jnp.int32, (span, QBLOCK), 0)
    query = first_row + lax.broadcasted_iota(jnp.int32, (span, QBLOCK), 1)
    allowed = (key >= starts_row) & (key <= query)
    return jnp.where(allowed, 0.0, MASK_FILL)


def per_span(first_ref, length, body):
    block = pl.program_id(0)
    seen = block - first_ref[block] + 1
    most = min(length, LONGEST + QBLOCK) // QBLOCK
    for blocks in range(1, most + 1):

        @pl.when(seen == blocks)
        def _(blocks=blocks):
            first_key = pl.multiple_of((block - blocks + 1) * QBLOCK, QBLOCK)
            body(blocks * QBLOCK, first_key, block * QBLOCK)


def attend_kernel(pairs, first_ref, q_ref, k_ref, v_ref, starts_ref, out_ref, lse_ref, v_turned, bias):
    @pl.when(pl.program_id(0) == 0)
    def _():
        v_turned[...] = jnp.transpose(v_ref[...])

    def body(span, first_key, first_row):
        bias[:span, :] = masked_bias(starts_ref[...], first_key, span, first_row)
        keys_at = pl.ds(first_key, span)
        lanes = [slice(pair * PAIR, (pair + 1) * PAIR) for pair in range(pairs)]
        scored, weighed = {}, {}
        for step in range(pairs + 2):
            if step < pairs:
                scored[step] = dot_nt(k_ref[keys_at, lanes[step]], split_heads(q_ref[:, lanes[step]])).astype(BF)
            pair = step - 2
            if pair >= 0:
                weights, total = weighed.pop(pair)
                both = dot_nn(v_turned[lanes[pair], keys_at], weights) * (1.0 / total)
                out_ref[:, lanes[pair]] = join_heads(both).astype(BF)
            pair = step - 1
            if 0 <= pair < pairs:
                fill = bias[:span, :]
                scores = scored.pop(pair).astype(F32) + jnp.concatenate([fill, fill], axis=1)
                top = jnp.max(scores, axis=0, keepdims=True)
                weights = jnp.exp(scores - top)
                total = jnp.sum(weights, axis=0, keepdims=True)
                lse_ref[0, pair : pair + 1, :] = top + jnp.log(total)
                weighed[pair] = (weights.astype(BF), total)

    per_span(first_ref, k_ref.shape[0], body)


def attend(queries, keys, values, starts, first):
    length, width = queries.shape
    pairs = width // PAIR
    blocks = length // QBLOCK
    block = pl.BlockSpec((QBLOCK, width), lambda i, f: (i, 0))
    return pl.pallas_call(
        functools.partial(attend_kernel, pairs),
        name="attend",
        out_shape=[
            jax.ShapeDtypeStruct((length, width), BF),
            jax.ShapeDtypeStruct((blocks, pairs, 2 * QBLOCK), F32),
        ],
        grid_spec=pltpu.PrefetchScalarGridSpec(
            num_scalar_prefetch=1,
            grid=(blocks,),
            in_specs=[
                block,
                whole((length, width)),
                whole((length, width)),
                pl.BlockSpec((1, QBLOCK), lambda i, f: (0, i)),
            ],
            out_specs=[block, pl.BlockSpec((1, pairs, 2 * QBLOCK), lambda i, f: (i, 0, 0))],
            scratch_shapes=[
                pltpu.VMEM((width, length), BF),
                pltpu.VMEM((min(length, LONGEST + QBLOCK), QBLOCK), F32),
            ],
        ),
        cost_estimate=cost(4 * length * length * width, 10 * length * width),
    )(first, queries, keys, values, starts)


def attend_back_kernel(
    pairs, first_ref, q_ref, k_ref, v_ref, g_ref, lse_ref, starts_ref, cos_ref, sin_ref, out_ref, k_turned, bias, dk, dv
):
    width = pairs * PAIR
    block = pl.program_id(0)

    @pl.when(block == 0)
    def _():
        k_turned[...] = jnp.transpose(k_ref[...])
        dk[...] = jnp.zeros_like(dk)
        dv[...] = jnp.zeros_like(dv)

    rows = pl.ds(pl.multiple_of(block * QBLOCK, QBLOCK), QBLOCK)
    cosine, sine = cos_ref[rows, :], sin_ref[rows, :]

    def body(span, first_key, first_row):
        bias[:span, :] = masked_bias(starts_ref[...], first_key, span, first_row)
        keys_at = pl.ds(first_key, span)
        lanes = [slice(pair * PAIR, (pair + 1) * PAIR) for pair in range(pairs)]
        scored, ready = {}, {}
        for step in range(pairs + 2):
            if step < pairs:
                at = lanes[step]
                queries, grads = split_heads(q_ref[:, at]), split_heads(g_ref[:, at])
                scores = dot_nt(k_ref[keys_at, at], queries).astype(BF)
                scored[step] = (scores, dot_nt(v_ref[keys_at, at], grads), queries, grads)
            pair = step - 2
            if pair >= 0:
                at = lanes[pair]
                probs, grad_scores, queries, grads = ready.pop(pair)
                dv[keys_at, at] += dot_nn(probs, grads)
                dk[keys_at, at] += dot_nn(grad_scores, queries)
                both = dot_nn(k_turned[at, keys_at], grad_scores)
                dq = (join_heads(both) * HEAD_DIM**-0.5).astype(BF).astype(F32)
                out_ref[rows, at] = (dq * cosine - swap_halves(dq) * sine).astype(BF)
            pair = step - 1
            if 0 <= pair < pairs:
                scores, grad_probs, queries, grads = scored.pop(pair)
                fill = bias[:span, :]
                scores = scores.astype(F32) + jnp.concatenate([fill, fill], axis=1)
                probs = jnp.exp(scores - lse_ref[0, pair : pair + 1, :])
                delta = jnp.sum(probs * grad_probs, axis=0, keepdims=True)
                ready[pair] = (probs.astype(BF), (probs * (grad_probs - delta)).astype(BF), queries, grads)

    per_span(first_ref, k_ref.shape[0], body)

    @pl.when(block == pl.num_programs(0) - 1)
    def _():
        def finish(step, carry):
            at = pl.ds(pl.multiple_of(step * QBLOCK, QBLOCK), QBLOCK)
            turn, slant = cos_ref[at, :], sin_ref[at, :]
            for pair in range(pairs):
                lanes = slice(pair * PAIR, (pair + 1) * PAIR)
                grad = dk[at, lanes].astype(BF).astype(F32)
                out_ref[at, width + pair * PAIR : width + (pair + 1) * PAIR] = (
                    grad * turn - swap_halves(grad) * slant
                ).astype(BF)
            out_ref[at, 2 * width : 3 * width] = dv[at, :].astype(BF)
            return carry

        lax.fori_loop(0, k_ref.shape[0] // QBLOCK, finish, 0)


def attend_back(queries, keys, values, grads, lse, starts, first, cosine, sine):
    length, width = queries.shape
    pairs = width // PAIR
    blocks = length // QBLOCK
    block = pl.BlockSpec((QBLOCK, width), lambda i, f: (i, 0))
    full = whole((length, width))
    table = whole((length, PAIR))
    return pl.pallas_call(
        functools.partial(attend_back_kernel, pairs),
        name="attend_back",
        out_shape=jax.ShapeDtypeStruct((length, 3 * width), BF),
        grid_spec=pltpu.PrefetchScalarGridSpec(
            num_scalar_prefetch=1,
            grid=(blocks,),
            in_specs=[
                block,
                full,
                full,
                block,
                pl.BlockSpec((1, pairs, 2 * QBLOCK), lambda i, f: (i, 0, 0)),
                pl.BlockSpec((1, QBLOCK), lambda i, f: (0, i)),
                table,
                table,
            ],
            out_specs=whole((length, 3 * width)),
            scratch_shapes=[
                pltpu.VMEM((width, length), BF),
                pltpu.VMEM((min(length, LONGEST + QBLOCK), QBLOCK), F32),
                pltpu.VMEM((length, width), F32),
                pltpu.VMEM((length, width), F32),
            ],
        ),
        cost_estimate=cost(10 * length * length * width, 16 * length * width),
    )(first, queries, keys, values, grads, lse, starts, cosine, sine)


def packed_slices(rows, down_rows, width, hidden_width):
    slices = [("down", (0, down_rows), (0, width), 0, 0), ("out", (0, rows), (0, width), down_rows, 0)]
    top = down_rows + rows
    both = 2 * hidden_width
    for at in range(0, both - width + 1, width):
        slices.append(("both", (0, rows), (at, at + width), top, 0))
        top += rows
    rest = both % width
    if rest:
        few = rows * rest // width
        for place in range(width // rest):
            slices.append(("both", (place * few, (place + 1) * few), (both - rest, both), top, place * rest))
        top += few
    return slices, top


def feed_copies(packed, targets, owner, sems):
    w_out, w_both, w_down = targets
    parts = w_out.shape[0] // packed[0]
    rows, down_rows = packed[0], w_down.shape[0] // parts
    slices, height = packed_slices(rows, down_rows, w_out.shape[1], w_down.shape[0])
    kinds = {"out": (w_out, rows, 0), "both": (w_both, rows, 1), "down": (w_down, down_rows, 2)}
    copies = {"out": [], "both": [], "down": []}
    for name, (low, high), (left, right), top, column in slices:
        target, each, number = kinds[name]
        source = packed[1].at[
            pl.ds(pl.multiple_of(owner * height + top, 16), high - low), column : column + right - left
        ]
        goal = target.at[pl.ds(pl.multiple_of(owner * each + low, 16), high - low), left:right]
        copies[name].append(pltpu.make_async_copy(source, goal, sems.at[number]))
    return copies


def feed_kernel(rows, count, width, hidden_width, *refs):
    x_ref, att_ref, dy_ref, gain_ref = refs[:4]
    given, refs = refs[4 : 4 + count], refs[4 + count :]
    y_ref, n_ref, hid_ref, dgate_ref, dup_ref, dm_ref, dmr_ref, datt_ref = refs[:8]
    w_out, w_both, w_down, result, back, sems = refs[8:]
    targets = (w_out, w_both, w_down)
    parts = width // rows

    def whole_copies():
        views = (w_out, w_both.at[:, :hidden_width], w_both.at[:, hidden_width:], w_down)
        return [pltpu.make_async_copy(piece, view, sems.at[0]) for piece, view in zip(given, views)]

    def per_owner(act):
        def step(owner, carry):
            act(feed_copies((rows, given[0]), targets, owner, sems))
            return carry

        lax.fori_loop(0, parts, step, 0)

    opening = pl.program_id(0) == 0

    @pl.when(opening)
    def _():
        if count > 1:
            copies = whole_copies()
            start_all(copies)
            wait_all(copies)
        else:
            per_owner(lambda copies: start_all(copies["out"]))
            per_owner(lambda copies: start_all(copies["both"] + copies["down"]))

    def wait_for(*kinds):
        if count == 1:

            @pl.when(opening)
            def _():
                per_owner(lambda copies: wait_all([copy for kind in kinds for copy in copies[kind]]))

    wait_for("out")
    gain = gain_ref[1:2, :]
    dy = dy_ref[...]
    middle = x_ref[...].astype(F32) + dot_nn(att_ref[...], w_out[...])
    inverse = lax.rsqrt(jnp.mean(middle * middle, axis=1, keepdims=True) + EPSILON)
    normed = (middle * inverse * gain).astype(BF)
    n_ref[...] = normed
    wait_for("both", "down")
    result[...] = middle
    back[...] = jnp.zeros_like(middle)
    step = min(FSTEP, hidden_width)

    def chunk(number, carry):
        at = pl.multiple_of(number * step, step)
        part = pl.ds(at, step)
        w_gate = w_both[:, part]
        w_up = w_both[:, pl.ds(pl.multiple_of(hidden_width + at, step), step)]
        gate = dot_nn(normed, w_gate)
        up = dot_nn(normed, w_up)
        dh = dot_nt(dy, w_down[part, :])
        sigma = 1.0 / (1.0 + jnp.exp(-gate))
        silu = gate * sigma
        hidden = (silu * up).astype(BF)
        hid_ref[:, part] = hidden
        dgate = (dh * up * (sigma * (1.0 + gate * (1.0 - sigma)))).astype(BF)
        dup = (dh * silu).astype(BF)
        dgate_ref[:, part] = dgate
        dup_ref[:, part] = dup
        result[...] += dot_nn(hidden, w_down[part, :])
        back[...] += dot_nt(dgate, w_gate) + dot_nt(dup, w_up)
        return carry

    lax.fori_loop(0, hidden_width // step, chunk, 0)
    y_ref[...] = result[...].astype(BF)
    scaled = back[...] * gain
    dm = dy.astype(F32) + inverse * scaled - middle * (inverse * inverse * inverse) * jnp.mean(
        scaled * middle, axis=1, keepdims=True
    )
    dm_ref[...] = dm
    dmr = dm.astype(BF)
    dmr_ref[...] = dmr
    datt_ref[...] = dot_nt(dmr, w_out[...]).astype(BF)


def feed(x, attended, dy, gain, given, rows, hidden_width):
    tokens, width = x.shape
    block = pl.BlockSpec((FBLOCK, width), lambda i: (i, 0))
    broad = pl.BlockSpec((FBLOCK, hidden_width), lambda i: (i, 0))
    narrow, large = jax.ShapeDtypeStruct((tokens, width), BF), jax.ShapeDtypeStruct((tokens, hidden_width), BF)
    return pl.pallas_call(
        functools.partial(feed_kernel, rows, len(given), width, hidden_width),
        name="feed",
        out_shape=[narrow, narrow, large, large, large, jax.ShapeDtypeStruct((tokens, width), F32), narrow, narrow],
        grid=(tokens // FBLOCK,),
        in_specs=[block, block, block, whole((8, width))] + [ANY] * len(given),
        out_specs=[block, block, broad, broad, broad, block, block, block],
        scratch_shapes=[
            pltpu.VMEM((width, width), BF),
            pltpu.VMEM((width, 2 * hidden_width), BF),
            pltpu.VMEM((hidden_width, width), BF),
            pltpu.VMEM((FBLOCK, width), F32),
            pltpu.VMEM((FBLOCK, width), F32),
            pltpu.SemaphoreType.DMA((3,)),
        ],
        cost_estimate=cost(4 * tokens * width * (width + 3 * hidden_width), 20 * tokens * width + 6 * tokens * hidden_width),
    )(x, attended, dy, gain, *given)


def dot_tn(left, right):
    return lax.dot_general(left, right, (((0,), (0,)), ((), ())), preferred_element_type=F32)


def write_pieces(parts, total, keep, send):
    if parts == 1:
        keep[...] = total[...].astype(BF)
        return
    rows = total.shape[0] // parts
    me = lax.axis_index("fsdp")
    for place in range(parts // 2):
        upper, y_bit = place % (parts // 4), place // (parts // 4)
        for core, out in enumerate((keep, send)):
            owner = lax.bitwise_xor(me, upper * 4 + y_bit * 2 + core)
            out[place] = total[pl.ds(pl.multiple_of(owner * rows, 16), rows), :].astype(BF)


def outer_kernel(parts, counts, edges, *refs):
    lefts = []
    for count in counts:
        lefts.append(refs[:count])
        refs = refs[count:]
    rights, outs, total = refs[: len(counts)], refs[len(counts) : -1], refs[-1]
    step = pl.program_id(0)
    low = 0
    for group, right, high in zip(lefts, rights, edges):

        @pl.when((step >= low) & (step < high))
        def _(group=group, right=right):
            row = 0
            for left in group:
                total[row : row + left.shape[1], :] = dot_tn(left[...], right[...])
                row += left.shape[1]

        low = high
    write_pieces(parts, total, *((outs + (None,))[:2]))


def outer_sums(parts, pairs, tile, name):
    edges, specs, low = [], [], 0
    for lefts, right in pairs:
        steps = right.shape[1] // tile
        specs.append(
            pl.BlockSpec(
                (right.shape[0], tile), lambda j, low=low, steps=steps: (0, jnp.clip(j - low, 0, steps - 1))
            )
        )
        low += steps
        edges.append(low)
    width = low * tile
    tokens = pairs[0][1].shape[0]
    rows = sum(left.shape[1] for left in pairs[0][0])
    every_left = [left for lefts, _ in pairs for left in lefts]
    shape = (rows, width) if parts == 1 else (parts // 2, rows // parts, width)
    out_block = (rows, tile) if parts == 1 else (parts // 2, rows // parts, tile)
    index = (lambda j: (0, j)) if parts == 1 else (lambda j: (0, 0, j))
    n_out = 1 if parts == 1 else 2
    return pl.pallas_call(
        functools.partial(outer_kernel, parts, tuple(len(lefts) for lefts, _ in pairs), tuple(edges)),
        name=name,
        out_shape=[jax.ShapeDtypeStruct(shape, BF)] * n_out,
        grid=(low,),
        in_specs=[whole(left.shape) for left in every_left] + specs,
        out_specs=[pl.BlockSpec(out_block, index)] * n_out,
        scratch_shapes=[pltpu.VMEM((rows, tile), F32)],
        cost_estimate=cost(2 * tokens * rows * width, 2 * tokens * (rows + width) + 2 * rows * width),
    )(*every_left, *[right for _, right in pairs])


def feed_grads_kernel(parts, steps, n_ref, dgate_ref, dup_ref, hid_any, dy_any, out_ref, hidden, dy, total, sems):
    step = pl.program_id(0)
    tile = out_ref.shape[2]
    width = n_ref.shape[1]
    copies = [pltpu.make_async_copy(hid_any, hidden, sems.at[0]), pltpu.make_async_copy(dy_any, dy, sems.at[1])]

    @pl.when(step == 0)
    def _():
        start_all(copies)

    for low, right in ((0, dgate_ref), (steps, dup_ref)):

        @pl.when((step >= low) & (step < low + steps))
        def _(right=right):
            out_ref[...] = dot_tn(n_ref[...], right[...]).astype(BF).reshape(out_ref.shape)

    @pl.when(step == 2 * steps)
    def _():
        wait_all(copies)
        each = hidden.shape[1] // 2
        for at in (0, each):
            grad = dot_tn(hidden[:, at : at + each], dy[...]).astype(BF)
            total[at * parts // hidden.shape[1] : (at + each) * parts // hidden.shape[1]] = grad.reshape(
                parts // 2, hidden.shape[1] // parts, width
            )

    for place in range(steps):

        @pl.when(step == 2 * steps + place)
        def _(place=place):
            unit = 16 * parts
            for group in range(tile // unit):
                rows = slice((place * tile // unit + group) * 16, (place * tile // unit + group + 1) * 16)
                for column in range(width // unit):
                    out_ref[:, column * 16 : (column + 1) * 16, group * unit : (group + 1) * unit] = total[
                        :, rows, column * unit : (column + 1) * unit
                    ]


def feed_grads(parts, normed, dgate, dup, hidden, dy):
    tokens, width = normed.shape
    hidden_width = hidden.shape[1]
    tile = min(TILE, hidden_width)
    steps = hidden_width // tile
    rows = width // parts
    return pl.pallas_call(
        functools.partial(feed_grads_kernel, parts, steps),
        name="feed_grads",
        out_shape=jax.ShapeDtypeStruct((parts, 3 * rows, hidden_width), BF),
        grid=(3 * steps,),
        in_specs=[
            whole((tokens, width)),
            pl.BlockSpec((tokens, tile), lambda j: (0, jnp.minimum(j, steps - 1))),
            pl.BlockSpec((tokens, tile), lambda j: (0, jnp.clip(j - steps, 0, steps - 1))),
            ANY,
            ANY,
        ],
        out_specs=pl.BlockSpec((parts, rows, tile), lambda j: (0, j // steps, j % steps)),
        scratch_shapes=[
            pltpu.VMEM((tokens, hidden_width), BF),
            pltpu.VMEM((tokens, width), BF),
            pltpu.VMEM((parts, hidden_width // parts, width), BF),
            pltpu.SemaphoreType.DMA((2,)),
        ],
        cost_estimate=cost(6 * tokens * width * hidden_width, 6 * tokens * (hidden_width + width)),
    )(normed, dgate, dup, hidden, dy)


def input_grad_kernel(places, width, *refs):
    count = len(places)
    x_ref, dm_ref, grads_ref, gains_ref = refs[:4]
    groups = [(piece, *place) for piece, place in zip(refs[4 : 4 + count], places)]
    out_ref, weights, sem = refs[4 + count :]

    @pl.when(pl.program_id(0) == 0)
    def _():
        copies = load_copies(groups, weights, sem)
        start_all(copies)
        wait_all(copies)

    x = x_ref[...].astype(F32)
    inverse = lax.rsqrt(jnp.mean(x * x, axis=1, keepdims=True) + EPSILON)
    scaled = dot_nt(grads_ref[...], weights[:, : 3 * width]) * gains_ref[0:1, :]
    out_ref[...] = (
        dm_ref[...]
        + inverse * scaled
        - x * (inverse * inverse * inverse) * jnp.mean(scaled * x, axis=1, keepdims=True)
    )


def input_grad(x, dm, grads, gains, groups):
    tokens, width = x.shape
    block = pl.BlockSpec((TBLOCK, width), lambda i: (i, 0))
    return pl.pallas_call(
        functools.partial(input_grad_kernel, [place for _, *place in groups], width),
        name="input_grad",
        out_shape=jax.ShapeDtypeStruct((tokens, width), F32),
        grid=(tokens // TBLOCK,),
        in_specs=[block, block, pl.BlockSpec((TBLOCK, 3 * width), lambda i: (i, 0)), whole((8, width))]
        + [ANY] * len(groups),
        out_specs=block,
        scratch_shapes=[
            pltpu.VMEM((width, columns_of(groups)), BF),
            pltpu.SemaphoreType.DMA,
        ],
        cost_estimate=cost(6 * tokens * width * width, 6 * width * width + 16 * tokens * width),
    )(x, dm, grads, gains, *[piece for piece, *_ in groups])


def flip(values, bits):
    count = lax.axis_size("fsdp")
    return lax.ppermute(values, "fsdp", [(i, i ^ bits) for i in range(count)])


def across(values):
    return lax.ppermute(values, "seq", [(0, 1), (1, 0)])


def aligned(rows, down_rows, width, hidden_width, count):
    rest = 2 * hidden_width % width
    return (
        count == 16
        and rows % 16 == 0
        and down_rows % 16 == 0
        and (rest == 0 or (width % rest == 0 and rows * rest % (16 * width) == 0))
    )


def gate(values, *others):
    return lax.optimization_barrier((values,) + others)[0]


def gather_rows(shard, parts):
    if parts == 1:
        return [(lax.all_gather(shard, "fsdp", axis=0, tiled=True), (0,), 0)]
    uppers = tuple(range(0, parts, 4))
    mine = jnp.concatenate([shard] + [flip(shard, upper) for upper in uppers[1:]])
    beside = flip(mine, 2)
    got = [(mine, 0, 0), (beside, 2, 0), (across(mine), 0, 1), (across(beside), 2, 1)]
    got += [(flip(piece, 1), low + 1, side) for piece, low, side in got]
    return [(piece, tuple(upper + low for upper in uppers), side) for piece, low, side in got]


def pack_kernel(q_ref, k_ref, v_ref, column_ref, out_ref, gate_ref, up_ref, down_ref, in_ref, packed_ref):
    rows, width = out_ref.shape
    hidden_width = gate_ref.shape[1]
    half = in_ref.shape[1]
    for rank in range(2):

        @pl.when(lax.axis_index("seq") == rank)
        def _(rank=rank):
            left = 0
            for piece in (q_ref, k_ref, v_ref, column_ref):
                start, stop = max(left, rank * half), min(left + piece.shape[1], (rank + 1) * half)
                if start < stop:
                    in_ref[:, start - rank * half : stop - rank * half] = piece[:, start - left : stop - left]
                left += piece.shape[1]

    slices, _ = packed_slices(rows, down_ref.shape[0], width, hidden_width)
    for name, (low, high), (left, right), top, column in slices:
        spans = {
            "down": [(down_ref, left, right, 0)],
            "out": [(out_ref, left, right, 0)],
            "both": [
                (gate_ref, left, min(right, hidden_width), 0),
                (up_ref, max(left, hidden_width), right, hidden_width),
            ],
        }[name]
        for array, start, stop, base in spans:
            if start < stop:
                packed_ref[top : top + high - low, column + start - left : column + stop - left] = array[
                    low:high, start - base : stop - base
                ]


def pack(w_query, w_key, w_value, column, w_out, w_gate, w_up, w_down):
    rows, width = w_out.shape
    _, height = packed_slices(rows, w_down.shape[0], width, w_gate.shape[1])
    given = (w_query, w_key, w_value, column, w_out, w_gate, w_up, w_down)
    return pl.pallas_call(
        pack_kernel,
        name="pack",
        out_shape=[
            jax.ShapeDtypeStruct((rows, (3 * width + column.shape[1]) // 2), BF),
            jax.ShapeDtypeStruct((height, width), BF),
        ],
    )(*given)


class Scatter:
    def __init__(self, outs, parts, rank):
        self.parts, self.rank = parts, rank
        if parts == 1:
            self.total = lax.psum_scatter(outs[0], "fsdp", scatter_dimension=0, tiled=True)
            return
        self.keep, send = outs
        self.got = flip(send, 1)
        self.half = self.keep.shape[2] // 2

    def columns(self, side, rows):
        at = lax.bitwise_xor(self.rank, side) * self.half
        kept, got = [lax.dynamic_slice_in_dim(array, at, self.half, 2)[rows] for array in (self.keep, self.got)]
        return kept.astype(F32) + got.astype(F32)

    def x_hop(self):
        if self.parts == 1:
            return []
        aside = self.columns(1, slice(None)).astype(BF)
        self.aside = across(aside)
        return [aside]

    def y_hop(self):
        if self.parts == 1:
            return []
        upper = slice(self.parts // 4, None)
        ahead = (self.columns(0, upper) + self.aside[upper].astype(F32)).astype(BF)
        self.ahead = flip(ahead, 2)
        return [ahead]

    def z_hop(self):
        if self.parts == 1:
            return []
        lower = slice(0, self.parts // 4)
        sums = self.columns(0, lower) + self.aside[lower].astype(F32) + self.ahead.astype(F32)
        self.own, sends = sums[0], [total.astype(BF) for total in sums[1:]]
        self.others = [flip(send, 4 * (j + 1)) for j, send in enumerate(sends)]
        return sends

    def result(self):
        if self.parts == 1:
            return self.total.astype(F32) + across(self.total).astype(F32)
        total = self.own
        for piece in self.others:
            total = total + piece.astype(F32)
        total = total.astype(BF)
        partner = across(total)
        first = jnp.where(self.rank == 0, total, partner)
        second = jnp.where(self.rank == 0, partner, total)
        return jnp.concatenate([first, second], axis=1).astype(F32)


def rope_tables(length):
    half = HEAD_DIM // 2
    inverse = jnp.exp(jnp.arange(half, dtype=F32) * (-2.0 * math.log(10000.0) / HEAD_DIM))
    low = jnp.arange(32, dtype=jnp.int32).astype(F32)[:, None] * inverse[None, :]
    high = (jnp.arange(length // 32, dtype=jnp.int32) * 32).astype(F32)[:, None] * inverse[None, :]
    cos_low, sin_low = jnp.cos(low)[None], jnp.sin(low)[None]
    cos_high, sin_high = jnp.cos(high)[:, None], jnp.sin(high)[:, None]
    cosine = (cos_high * cos_low - sin_high * sin_low).reshape(length, half)
    sine = (sin_high * cos_low + cos_high * sin_low).reshape(length, half)
    return (
        jnp.concatenate([cosine] * 4, axis=1),
        jnp.concatenate([-sine, sine, -sine, sine], axis=1),
    )


def per_device(
    tokens, doc_ids, cotangent, w_query, w_key, w_value, w_out, w_gate, w_up, w_down, gain_attn, gain_ffn
):
    seq_rank = lax.axis_index("seq")
    count = lax.axis_size("fsdp")
    micro, _, span, width = tokens.shape
    hidden_width = w_gate.shape[1]
    rows = w_query.shape[0]
    parts = count if aligned(rows, w_down.shape[0], width, hidden_width, count) else 1

    column = jnp.pad(jnp.stack([gain_attn, gain_ffn], axis=1), ((0, 0), (0, 254)))
    if parts == 1:
        w_in = jnp.concatenate([w_query, w_key, w_value, column], axis=1)
        given = [lax.all_gather(weight, "fsdp", axis=0, tiled=True) for weight in (w_out, w_gate, w_up, w_down)]
    else:
        w_in, packed = pack(w_query, w_key, w_value, column, w_out, w_gate, w_up, w_down)
        given = [lax.all_gather(packed, "fsdp", axis=0, tiled=True)]

    def exchanged(array):
        own = lax.dynamic_index_in_dim(array, seq_rank, 0, keepdims=False)[0]
        return own, lax.dynamic_index_in_dim(array, 1 - seq_rank, 0, keepdims=False)[0]

    def ordered(own, other):
        return jnp.where(seq_rank == 0, jnp.concatenate([own, other]), jnp.concatenate([other, own]))

    def halves(array):
        own = lax.dynamic_slice_in_dim(array, seq_rank * span, span, 0)
        other = lax.dynamic_slice_in_dim(array, (1 - seq_rank) * span, span, 0)
        return own, other

    def give_back(own, other):
        first, second = jnp.where(seq_rank == 0, own, other), jnp.where(seq_rank == 0, other, own)
        return jnp.stack([first, second])[:, None]

    groups_in = gather_rows(w_in, parts)
    own_x, other_x = exchanged(tokens)
    x = ordered(own_x, across(other_x))
    own_docs, other_docs = exchanged(doc_ids)
    docs = ordered(own_docs, across(other_docs))
    own_dy, other_dy = exchanged(gate(cotangent, x, *[piece for piece, *_ in groups_in]))
    dy = ordered(own_dy, across(other_dy))

    length = x.shape[0]
    cosine, sine = rope_tables(length)
    starts = jnp.sum((docs[None, :] < docs[:, None]).astype(jnp.int32), axis=1)
    first = starts[::QBLOCK] // QBLOCK
    starts = starts[None, :]

    normed, queries, keys, values, gains = project(x, cosine, sine, groups_in)
    attended, lse = attend(queries, keys, values, starts, first)
    y, normed_two, hidden, dgate, dup, dm, dmr, datt = feed(
        x, attended, dy, gains, given, rows if parts > 1 else width, hidden_width
    )
    own_y, other_y = halves(y)
    output = give_back(own_y, across(other_y))

    if parts == 1:
        sum_gate, sum_up, sum_down = [
            lax.psum_scatter(outer_sums(1, [(lefts, right)], tile, name)[0], "fsdp", scatter_dimension=0, tiled=True)
            for lefts, right, tile, name in (
                ([normed_two], dgate, 512, "grad_gate"),
                ([normed_two], dup, 512, "grad_up"),
                ([hidden], dy, width // 2, "grad_down"),
            )
        ]
        sums = (sum_gate, sum_up, sum_down)
    else:
        ff = feed_grads(parts, normed_two, dgate, dup, hidden, dy)
        datt = gate(datt, ff)
        ff = lax.psum_scatter(ff.reshape(-1, hidden_width), "fsdp", scatter_dimension=0, tiled=True)
        sums = (ff,)
    grads = attend_back(queries, keys, values, datt, lse, starts, first, cosine, sine)
    scatter = Scatter(
        outer_sums(parts, [([normed], grads), ([attended], dmr)], width, "grad_in"), parts, seq_rank
    )
    sent = scatter.x_hop()
    grad_x = input_grad(gate(x, *sent), dm, grads, gains, groups_in)
    own_g, other_g = halves(grad_x)
    sent = scatter.y_hop()
    grad_tokens = give_back(own_g, across(gate(other_g.astype(BF), *sent)).astype(F32))
    scatter.z_hop()
    sum_in = scatter.result()
    sums = [part.astype(F32) + across(part).astype(F32) for part in sums]
    if parts == 1:
        sum_gate, sum_up, sum_down = sums
    else:
        sum_gate, sum_up, rest = sums[0][:rows], sums[0][rows : 2 * rows], sums[0][2 * rows :]
        unit = 16 * parts
        rest = rest.reshape(rows // 16, 16, hidden_width // unit, unit)
        sum_down = rest.transpose(2, 1, 0, 3).reshape(w_down.shape)

    sum_in, sum_out = sum_in[:, : 3 * width], sum_in[:, 3 * width :]
    grad_gain_attn = sum(
        jnp.sum(weight.astype(F32) * sum_in[:, at * width : (at + 1) * width], axis=1)
        for at, weight in enumerate((w_query, w_key, w_value))
    ) / gain_attn.astype(F32)
    grad_gain_ffn = (
        jnp.sum(w_gate.astype(F32) * sum_gate, axis=1) + jnp.sum(w_up.astype(F32) * sum_up, axis=1)
    ) / gain_ffn.astype(F32)
    by_part = [sum_in[:, at * width : (at + 1) * width] for at in range(3)]
    return (output, grad_tokens, *by_part, sum_out, sum_gate, sum_up, sum_down, grad_gain_attn, grad_gain_ffn)


def solution(mesh):
    rows = P("fsdp", None)
    acts = P(None, "fsdp", "seq", None)
    return jax.shard_map(
        per_device,
        mesh=mesh,
        in_specs=(acts, P(None, "fsdp", "seq"), acts) + (rows,) * 7 + (P("fsdp"),) * 2,
        out_specs=(acts, acts) + (rows,) * 7 + (P("fsdp"),) * 2,
        check_vma=False,
    )
```

```python
import functools
import math

import jax
import jax.numpy as jnp
from jax import lax
from jax.experimental import pallas as pl
from jax.experimental.pallas import tpu as pltpu
from jax.sharding import PartitionSpec as P

HEAD_DIM = 64
EPSILON = 1e-05
MASK_FILL = -1e30
LONGEST = 512
PAIR = 2 * HEAD_DIM
QBLOCK = 128
TBLOCK = 512
FBLOCK = 512
FSTEP = 512
TILE = 1024
BF = jnp.bfloat16
F32 = jnp.float32
ANY = pl.BlockSpec(memory_space=pl.ANY)


def cost(flops, nbytes, trans=0):
    return pl.CostEstimate(flops=int(flops), bytes_accessed=int(nbytes), transcendentals=int(trans))


def whole(shape):
    zeros = (0,) * len(shape)
    return pl.BlockSpec(shape, lambda *_: zeros)


def dot_nt(left, right):
    return lax.dot_general(left, right, (((1,), (1,)), ((), ())), preferred_element_type=F32)


def dot_nn(left, right):
    return lax.dot_general(left, right, (((1,), (0,)), ((), ())), preferred_element_type=F32)


def swap_halves(values):
    lane = lax.broadcasted_iota(jnp.int32, values.shape, 1)
    width = values.shape[1]
    half = HEAD_DIM // 2
    ahead = pltpu.roll(values, width - half, 1)
    behind = pltpu.roll(values, half, 1)
    return jnp.where((lane & (HEAD_DIM - 1)) < half, ahead, behind)


def wide(table, width):
    return jnp.concatenate([table] * (width // table.shape[1]), axis=1)


def load_copies(groups, scratch, sem):
    if len(groups) == 1:
        return [pltpu.make_async_copy(groups[0][0], scratch, sem)]
    me, rank = lax.axis_index("fsdp"), lax.axis_index("seq")
    rows = 2 * scratch.shape[0] // sum(len(places) for _, places, _ in groups)
    half = scratch.shape[1] // 2
    copies = []
    for piece, places, side in groups:
        columns = pl.ds(pl.multiple_of(lax.bitwise_xor(rank, side) * half, 128), half)
        for at, place in enumerate(places):
            target = pl.ds(pl.multiple_of(lax.bitwise_xor(me, place) * rows, 16), rows)
            copies.append(
                pltpu.make_async_copy(piece.at[pl.ds(at * rows, rows), :], scratch.at[target, columns], sem)
            )
    return copies


def columns_of(groups):
    return groups[0][0].shape[1] * (1 if len(groups) == 1 else 2)


def start_all(copies):
    for copy in copies:
        copy.start()


def wait_all(copies):
    for copy in copies:
        copy.wait()


def rows_of(block):
    return jnp.transpose(block.astype(F32))[0:8, :]


def project_kernel(places, width, *refs):
    x_ref, cos_ref, sin_ref = refs[:3]
    count = len(places)
    groups = [(piece, *place) for piece, place in zip(refs[3 : 3 + count], places)]
    n_ref, q_ref, k_ref, v_ref, gains_ref = refs[3 + count : 8 + count]
    weights, gain, sem = refs[8 + count :]

    @pl.when(pl.program_id(0) == 0)
    def _():
        copies = load_copies(groups, weights, sem)
        start_all(copies)
        wait_all(copies)
        gain[...] = rows_of(weights[:, 3 * width : 3 * width + 128])
        gains_ref[...] = gain[...]

    x = x_ref[...].astype(F32)
    inverse = lax.rsqrt(jnp.mean(x * x, axis=1, keepdims=True) + EPSILON)
    normed = (x * inverse * gain[0:1, :]).astype(BF)
    n_ref[...] = normed
    cosine, sine = wide(cos_ref[...], width // 2), wide(sin_ref[...], width // 2)
    for part, out in enumerate((q_ref, k_ref)):
        for at in range(0, width, width // 2):
            linear = dot_nn(normed, weights[:, part * width + at : part * width + at + width // 2])
            turned = (linear * cosine + swap_halves(linear) * sine).astype(BF)
            if part == 0:
                turned = turned * jnp.asarray(HEAD_DIM**-0.5, BF)
            out[:, at : at + width // 2] = turned
    v_ref[...] = dot_nn(normed, weights[:, 2 * width : 3 * width]).astype(BF)


def project(x, cosine, sine, groups):
    tokens, width = x.shape
    total = columns_of(groups)
    shape = jax.ShapeDtypeStruct((tokens, width), BF)
    block = pl.BlockSpec((TBLOCK, width), lambda i: (i, 0))
    table = pl.BlockSpec((TBLOCK, PAIR), lambda i: (i, 0))
    return pl.pallas_call(
        functools.partial(project_kernel, [place for _, *place in groups], width),
        name="project",
        out_shape=[shape] * 4 + [jax.ShapeDtypeStruct((8, width), F32)],
        grid=(tokens // TBLOCK,),
        in_specs=[block, table, table] + [ANY] * len(groups),
        out_specs=[block] * 4 + [whole((8, width))],
        scratch_shapes=[
            pltpu.VMEM((width, total), BF),
            pltpu.VMEM((8, width), F32),
            pltpu.SemaphoreType.DMA,
        ],
        cost_estimate=cost(6 * tokens * width * width, 6 * width * width + 10 * tokens * width),
    )(x, cosine, sine, *[piece for piece, *_ in groups])


def split_heads(values):
    lane = lax.broadcasted_iota(jnp.int32, values.shape, 1)
    zero = jnp.zeros_like(values)
    return jnp.concatenate(
        [jnp.where(lane < HEAD_DIM, values, zero), jnp.where(lane < HEAD_DIM, zero, values)], axis=0
    )


def join_heads(both):
    rows = both.shape[1] // 2
    own = jnp.concatenate([both[:HEAD_DIM, :rows], both[HEAD_DIM:, rows:]], axis=0)
    return jnp.transpose(own)


def masked_bias(starts_row, first_key, span, first_row):
    key = first_key + lax.broadcasted_iota(jnp.int32, (span, QBLOCK), 0)
    query = first_row + lax.broadcasted_iota(jnp.int32, (span, QBLOCK), 1)
    allowed = (key >= starts_row) & (key <= query)
    return jnp.where(allowed, 0.0, MASK_FILL)


def per_span(first_ref, length, body):
    block = pl.program_id(0)
    seen = block - first_ref[block] + 1
    most = min(length, LONGEST + QBLOCK) // QBLOCK
    for blocks in range(1, most + 1):

        @pl.when(seen == blocks)
        def _(blocks=blocks):
            first_key = pl.multiple_of((block - blocks + 1) * QBLOCK, QBLOCK)
            body(blocks * QBLOCK, first_key, block * QBLOCK)


def attend_kernel(pairs, first_ref, q_ref, k_ref, v_ref, starts_ref, out_ref, lse_ref, v_turned, bias):
    @pl.when(pl.program_id(0) == 0)
    def _():
        v_turned[...] = jnp.transpose(v_ref[...])

    def body(span, first_key, first_row):
        bias[:span, :] = masked_bias(starts_ref[...], first_key, span, first_row)
        keys_at = pl.ds(first_key, span)
        lanes = [slice(pair * PAIR, (pair + 1) * PAIR) for pair in range(pairs)]
        scored, weighed = {}, {}
        for step in range(pairs + 2):
            if step < pairs:
                scored[step] = dot_nt(k_ref[keys_at, lanes[step]], split_heads(q_ref[:, lanes[step]])).astype(BF)
            pair = step - 2
            if pair >= 0:
                weights, total = weighed.pop(pair)
                both = dot_nn(v_turned[lanes[pair], keys_at], weights) * (1.0 / total)
                out_ref[:, lanes[pair]] = join_heads(both).astype(BF)
            pair = step - 1
            if 0 <= pair < pairs:
                fill = bias[:span, :]
                scores = scored.pop(pair).astype(F32) + jnp.concatenate([fill, fill], axis=1)
                top = jnp.max(scores, axis=0, keepdims=True)
                weights = jnp.exp(scores - top)
                total = jnp.sum(weights, axis=0, keepdims=True)
                lse_ref[0, pair : pair + 1, :] = top + jnp.log(total)
                weighed[pair] = (weights.astype(BF), total)

    per_span(first_ref, k_ref.shape[0], body)


def attend(queries, keys, values, starts, first):
    length, width = queries.shape
    pairs = width // PAIR
    blocks = length // QBLOCK
    block = pl.BlockSpec((QBLOCK, width), lambda i, f: (i, 0))
    return pl.pallas_call(
        functools.partial(attend_kernel, pairs),
        name="attend",
        out_shape=[
            jax.ShapeDtypeStruct((length, width), BF),
            jax.ShapeDtypeStruct((blocks, pairs, 2 * QBLOCK), F32),
        ],
        grid_spec=pltpu.PrefetchScalarGridSpec(
            num_scalar_prefetch=1,
            grid=(blocks,),
            in_specs=[
                block,
                whole((length, width)),
                whole((length, width)),
                pl.BlockSpec((1, QBLOCK), lambda i, f: (0, i)),
            ],
            out_specs=[block, pl.BlockSpec((1, pairs, 2 * QBLOCK), lambda i, f: (i, 0, 0))],
            scratch_shapes=[
                pltpu.VMEM((width, length), BF),
                pltpu.VMEM((min(length, LONGEST + QBLOCK), QBLOCK), F32),
            ],
        ),
        cost_estimate=cost(4 * length * length * width, 10 * length * width),
    )(first, queries, keys, values, starts)


def attend_back_kernel(
    pairs, first_ref, q_ref, k_ref, v_ref, g_ref, lse_ref, starts_ref, cos_ref, sin_ref, out_ref, k_turned, bias, dk, dv
):
    width = pairs * PAIR
    block = pl.program_id(0)

    @pl.when(block == 0)
    def _():
        k_turned[...] = jnp.transpose(k_ref[...])
        dk[...] = jnp.zeros_like(dk)
        dv[...] = jnp.zeros_like(dv)

    rows = pl.ds(pl.multiple_of(block * QBLOCK, QBLOCK), QBLOCK)
    cosine, sine = cos_ref[rows, :], sin_ref[rows, :]

    def body(span, first_key, first_row):
        bias[:span, :] = masked_bias(starts_ref[...], first_key, span, first_row)
        keys_at = pl.ds(first_key, span)
        lanes = [slice(pair * PAIR, (pair + 1) * PAIR) for pair in range(pairs)]
        scored, ready = {}, {}
        for step in range(pairs + 2):
            if step < pairs:
                at = lanes[step]
                queries, grads = split_heads(q_ref[:, at]), split_heads(g_ref[:, at])
                scores = dot_nt(k_ref[keys_at, at], queries).astype(BF)
                scored[step] = (scores, dot_nt(v_ref[keys_at, at], grads), queries, grads)
            pair = step - 2
            if pair >= 0:
                at = lanes[pair]
                probs, grad_scores, queries, grads = ready.pop(pair)
                dv[keys_at, at] += dot_nn(probs, grads)
                dk[keys_at, at] += dot_nn(grad_scores, queries)
                both = dot_nn(k_turned[at, keys_at], grad_scores)
                dq = (join_heads(both) * HEAD_DIM**-0.5).astype(BF).astype(F32)
                out_ref[rows, at] = (dq * cosine - swap_halves(dq) * sine).astype(BF)
            pair = step - 1
            if 0 <= pair < pairs:
                scores, grad_probs, queries, grads = scored.pop(pair)
                fill = bias[:span, :]
                scores = scores.astype(F32) + jnp.concatenate([fill, fill], axis=1)
                probs = jnp.exp(scores - lse_ref[0, pair : pair + 1, :])
                delta = jnp.sum(probs * grad_probs, axis=0, keepdims=True)
                ready[pair] = (probs.astype(BF), (probs * (grad_probs - delta)).astype(BF), queries, grads)

    per_span(first_ref, k_ref.shape[0], body)

    @pl.when(block == pl.num_programs(0) - 1)
    def _():
        def finish(step, carry):
            at = pl.ds(pl.multiple_of(step * QBLOCK, QBLOCK), QBLOCK)
            turn, slant = cos_ref[at, :], sin_ref[at, :]
            for pair in range(pairs):
                lanes = slice(pair * PAIR, (pair + 1) * PAIR)
                grad = dk[at, lanes].astype(BF).astype(F32)
                out_ref[at, width + pair * PAIR : width + (pair + 1) * PAIR] = (
                    grad * turn - swap_halves(grad) * slant
                ).astype(BF)
            out_ref[at, 2 * width : 3 * width] = dv[at, :].astype(BF)
            return carry

        lax.fori_loop(0, k_ref.shape[0] // QBLOCK, finish, 0)


def attend_back(queries, keys, values, grads, lse, starts, first, cosine, sine):
    length, width = queries.shape
    pairs = width // PAIR
    blocks = length // QBLOCK
    block = pl.BlockSpec((QBLOCK, width), lambda i, f: (i, 0))
    full = whole((length, width))
    table = whole((length, PAIR))
    return pl.pallas_call(
        functools.partial(attend_back_kernel, pairs),
        name="attend_back",
        out_shape=jax.ShapeDtypeStruct((length, 3 * width), BF),
        grid_spec=pltpu.PrefetchScalarGridSpec(
            num_scalar_prefetch=1,
            grid=(blocks,),
            in_specs=[
                block,
                full,
                full,
                block,
                pl.BlockSpec((1, pairs, 2 * QBLOCK), lambda i, f: (i, 0, 0)),
                pl.BlockSpec((1, QBLOCK), lambda i, f: (0, i)),
                table,
                table,
            ],
            out_specs=whole((length, 3 * width)),
            scratch_shapes=[
                pltpu.VMEM((width, length), BF),
                pltpu.VMEM((min(length, LONGEST + QBLOCK), QBLOCK), F32),
                pltpu.VMEM((length, width), F32),
                pltpu.VMEM((length, width), F32),
            ],
        ),
        cost_estimate=cost(10 * length * length * width, 16 * length * width),
    )(first, queries, keys, values, grads, lse, starts, cosine, sine)


def packed_slices(rows, down_rows, width, hidden_width):
    slices = [("down", (0, down_rows), (0, width), 0, 0), ("out", (0, rows), (0, width), down_rows, 0)]
    top = down_rows + rows
    both = 2 * hidden_width
    for at in range(0, both - width + 1, width):
        slices.append(("both", (0, rows), (at, at + width), top, 0))
        top += rows
    rest = both % width
    if rest:
        few = rows * rest // width
        for place in range(width // rest):
            slices.append(("both", (place * few, (place + 1) * few), (both - rest, both), top, place * rest))
        top += few
    return slices, top


def feed_copies(packed, targets, owner, sems):
    w_out, w_both, w_down = targets
    parts = w_out.shape[0] // packed[0]
    rows, down_rows = packed[0], w_down.shape[0] // parts
    slices, height = packed_slices(rows, down_rows, w_out.shape[1], w_down.shape[0])
    kinds = {"out": (w_out, rows, 0), "both": (w_both, rows, 1), "down": (w_down, down_rows, 2)}
    copies = {"out": [], "both": [], "down": []}
    for name, (low, high), (left, right), top, column in slices:
        target, each, number = kinds[name]
        source = packed[1].at[
            pl.ds(pl.multiple_of(owner * height + top, 16), high - low), column : column + right - left
        ]
        goal = target.at[pl.ds(pl.multiple_of(owner * each + low, 16), high - low), left:right]
        copies[name].append(pltpu.make_async_copy(source, goal, sems.at[number]))
    return copies


def feed_kernel(rows, count, width, hidden_width, *refs):
    x_ref, att_ref, dy_ref, gain_ref = refs[:4]
    given, refs = refs[4 : 4 + count], refs[4 + count :]
    y_ref, n_ref, hid_ref, dgate_ref, dup_ref, dm_ref, dmr_ref, datt_ref = refs[:8]
    w_out, w_both, w_down, result, back, sems = refs[8:]
    targets = (w_out, w_both, w_down)
    parts = width // rows

    def whole_copies():
        views = (w_out, w_both.at[:, :hidden_width], w_both.at[:, hidden_width:], w_down)
        return [pltpu.make_async_copy(piece, view, sems.at[0]) for piece, view in zip(given, views)]

    def per_owner(act):
        def step(owner, carry):
            act(feed_copies((rows, given[0]), targets, owner, sems))
            return carry

        lax.fori_loop(0, parts, step, 0)

    opening = pl.program_id(0) == 0

    @pl.when(opening)
    def _():
        if count > 1:
            copies = whole_copies()
            start_all(copies)
            wait_all(copies)
        else:
            per_owner(lambda copies: start_all(copies["out"]))
            per_owner(lambda copies: start_all(copies["both"] + copies["down"]))

    def wait_for(*kinds):
        if count == 1:

            @pl.when(opening)
            def _():
                per_owner(lambda copies: wait_all([copy for kind in kinds for copy in copies[kind]]))

    wait_for("out")
    gain = gain_ref[1:2, :]
    dy = dy_ref[...]
    middle = x_ref[...].astype(F32) + dot_nn(att_ref[...], w_out[...])
    inverse = lax.rsqrt(jnp.mean(middle * middle, axis=1, keepdims=True) + EPSILON)
    normed = (middle * inverse * gain).astype(BF)
    n_ref[...] = normed
    wait_for("both", "down")
    result[...] = middle
    back[...] = jnp.zeros_like(middle)
    step = min(FSTEP, hidden_width)

    def chunk(number, carry):
        at = pl.multiple_of(number * step, step)
        part = pl.ds(at, step)
        w_gate = w_both[:, part]
        w_up = w_both[:, pl.ds(pl.multiple_of(hidden_width + at, step), step)]
        gate = dot_nn(normed, w_gate)
        up = dot_nn(normed, w_up)
        dh = dot_nt(dy, w_down[part, :])
        sigma = 1.0 / (1.0 + jnp.exp(-gate))
        silu = gate * sigma
        hidden = (silu * up).astype(BF)
        hid_ref[:, part] = hidden
        dgate = (dh * up * (sigma * (1.0 + gate * (1.0 - sigma)))).astype(BF)
        dup = (dh * silu).astype(BF)
        dgate_ref[:, part] = dgate
        dup_ref[:, part] = dup
        result[...] += dot_nn(hidden, w_down[part, :])
        back[...] += dot_nt(dgate, w_gate) + dot_nt(dup, w_up)
        return carry

    lax.fori_loop(0, hidden_width // step, chunk, 0)
    y_ref[...] = result[...].astype(BF)
    scaled = back[...] * gain
    dm = dy.astype(F32) + inverse * scaled - middle * (inverse * inverse * inverse) * jnp.mean(
        scaled * middle, axis=1, keepdims=True
    )
    dm_ref[...] = dm
    dmr = dm.astype(BF)
    dmr_ref[...] = dmr
    datt_ref[...] = dot_nt(dmr, w_out[...]).astype(BF)


def feed(x, attended, dy, gain, given, rows, hidden_width):
    tokens, width = x.shape
    block = pl.BlockSpec((FBLOCK, width), lambda i: (i, 0))
    broad = pl.BlockSpec((FBLOCK, hidden_width), lambda i: (i, 0))
    narrow, large = jax.ShapeDtypeStruct((tokens, width), BF), jax.ShapeDtypeStruct((tokens, hidden_width), BF)
    return pl.pallas_call(
        functools.partial(feed_kernel, rows, len(given), width, hidden_width),
        name="feed",
        out_shape=[narrow, narrow, large, large, large, jax.ShapeDtypeStruct((tokens, width), F32), narrow, narrow],
        grid=(tokens // FBLOCK,),
        in_specs=[block, block, block, whole((8, width))] + [ANY] * len(given),
        out_specs=[block, block, broad, broad, broad, block, block, block],
        scratch_shapes=[
            pltpu.VMEM((width, width), BF),
            pltpu.VMEM((width, 2 * hidden_width), BF),
            pltpu.VMEM((hidden_width, width), BF),
            pltpu.VMEM((FBLOCK, width), F32),
            pltpu.VMEM((FBLOCK, width), F32),
            pltpu.SemaphoreType.DMA((3,)),
        ],
        cost_estimate=cost(4 * tokens * width * (width + 3 * hidden_width), 20 * tokens * width + 6 * tokens * hidden_width),
    )(x, attended, dy, gain, *given)


def dot_tn(left, right):
    return lax.dot_general(left, right, (((0,), (0,)), ((), ())), preferred_element_type=F32)


def write_pieces(parts, total, keep, send):
    if parts == 1:
        keep[...] = total[...].astype(BF)
        return
    rows = total.shape[0] // parts
    me = lax.axis_index("fsdp")
    for place in range(parts // 2):
        upper, y_bit = place % (parts // 4), place // (parts // 4)
        for core, out in enumerate((keep, send)):
            owner = lax.bitwise_xor(me, upper * 4 + y_bit * 2 + core)
            out[place] = total[pl.ds(pl.multiple_of(owner * rows, 16), rows), :].astype(BF)


def outer_kernel(parts, counts, edges, *refs):
    lefts = []
    for count in counts:
        lefts.append(refs[:count])
        refs = refs[count:]
    rights, outs, total = refs[: len(counts)], refs[len(counts) : -1], refs[-1]
    step = pl.program_id(0)
    low = 0
    for group, right, high in zip(lefts, rights, edges):

        @pl.when((step >= low) & (step < high))
        def _(group=group, right=right):
            row = 0
            for left in group:
                total[row : row + left.shape[1], :] = dot_tn(left[...], right[...])
                row += left.shape[1]

        low = high
    write_pieces(parts, total, *((outs + (None,))[:2]))


def outer_sums(parts, pairs, tile, name):
    edges, specs, low = [], [], 0
    for lefts, right in pairs:
        steps = right.shape[1] // tile
        specs.append(
            pl.BlockSpec(
                (right.shape[0], tile), lambda j, low=low, steps=steps: (0, jnp.clip(j - low, 0, steps - 1))
            )
        )
        low += steps
        edges.append(low)
    width = low * tile
    tokens = pairs[0][1].shape[0]
    rows = sum(left.shape[1] for left in pairs[0][0])
    every_left = [left for lefts, _ in pairs for left in lefts]
    shape = (rows, width) if parts == 1 else (parts // 2, rows // parts, width)
    out_block = (rows, tile) if parts == 1 else (parts // 2, rows // parts, tile)
    index = (lambda j: (0, j)) if parts == 1 else (lambda j: (0, 0, j))
    n_out = 1 if parts == 1 else 2
    return pl.pallas_call(
        functools.partial(outer_kernel, parts, tuple(len(lefts) for lefts, _ in pairs), tuple(edges)),
        name=name,
        out_shape=[jax.ShapeDtypeStruct(shape, BF)] * n_out,
        grid=(low,),
        in_specs=[whole(left.shape) for left in every_left] + specs,
        out_specs=[pl.BlockSpec(out_block, index)] * n_out,
        scratch_shapes=[pltpu.VMEM((rows, tile), F32)],
        cost_estimate=cost(2 * tokens * rows * width, 2 * tokens * (rows + width) + 2 * rows * width),
    )(*every_left, *[right for _, right in pairs])


def feed_grads_kernel(parts, steps, n_ref, dgate_ref, dup_ref, hid_any, dy_any, out_ref, hidden, dy, total, sems):
    step = pl.program_id(0)
    tile = out_ref.shape[2]
    width = n_ref.shape[1]
    copies = [pltpu.make_async_copy(hid_any, hidden, sems.at[0]), pltpu.make_async_copy(dy_any, dy, sems.at[1])]

    @pl.when(step == 0)
    def _():
        start_all(copies)

    for low, right in ((0, dgate_ref), (steps, dup_ref)):

        @pl.when((step >= low) & (step < low + steps))
        def _(right=right):
            out_ref[...] = dot_tn(n_ref[...], right[...]).astype(BF).reshape(out_ref.shape)

    @pl.when(step == 2 * steps)
    def _():
        wait_all(copies)
        each = hidden.shape[1] // 2
        for at in (0, each):
            grad = dot_tn(hidden[:, at : at + each], dy[...]).astype(BF)
            total[at * parts // hidden.shape[1] : (at + each) * parts // hidden.shape[1]] = grad.reshape(
                parts // 2, hidden.shape[1] // parts, width
            )

    for place in range(steps):

        @pl.when(step == 2 * steps + place)
        def _(place=place):
            unit = 16 * parts
            for group in range(tile // unit):
                rows = slice((place * tile // unit + group) * 16, (place * tile // unit + group + 1) * 16)
                for column in range(width // unit):
                    out_ref[:, column * 16 : (column + 1) * 16, group * unit : (group + 1) * unit] = total[
                        :, rows, column * unit : (column + 1) * unit
                    ]


def feed_grads(parts, normed, dgate, dup, hidden, dy):
    tokens, width = normed.shape
    hidden_width = hidden.shape[1]
    tile = min(TILE, hidden_width)
    steps = hidden_width // tile
    rows = width // parts
    return pl.pallas_call(
        functools.partial(feed_grads_kernel, parts, steps),
        name="feed_grads",
        out_shape=jax.ShapeDtypeStruct((parts, 3 * rows, hidden_width), BF),
        grid=(3 * steps,),
        in_specs=[
            whole((tokens, width)),
            pl.BlockSpec((tokens, tile), lambda j: (0, jnp.minimum(j, steps - 1))),
            pl.BlockSpec((tokens, tile), lambda j: (0, jnp.clip(j - steps, 0, steps - 1))),
            ANY,
            ANY,
        ],
        out_specs=pl.BlockSpec((parts, rows, tile), lambda j: (0, j // steps, j % steps)),
        scratch_shapes=[
            pltpu.VMEM((tokens, hidden_width), BF),
            pltpu.VMEM((tokens, width), BF),
            pltpu.VMEM((parts, hidden_width // parts, width), BF),
            pltpu.SemaphoreType.DMA((2,)),
        ],
        cost_estimate=cost(6 * tokens * width * hidden_width, 6 * tokens * (hidden_width + width)),
    )(normed, dgate, dup, hidden, dy)


def input_grad_kernel(places, width, *refs):
    count = len(places)
    x_ref, dm_ref, grads_ref, gains_ref = refs[:4]
    groups = [(piece, *place) for piece, place in zip(refs[4 : 4 + count], places)]
    out_ref, weights, sem = refs[4 + count :]

    @pl.when(pl.program_id(0) == 0)
    def _():
        copies = load_copies(groups, weights, sem)
        start_all(copies)
        wait_all(copies)

    x = x_ref[...].astype(F32)
    inverse = lax.rsqrt(jnp.mean(x * x, axis=1, keepdims=True) + EPSILON)
    scaled = dot_nt(grads_ref[...], weights[:, : 3 * width]) * gains_ref[0:1, :]
    out_ref[...] = (
        dm_ref[...]
        + inverse * scaled
        - x * (inverse * inverse * inverse) * jnp.mean(scaled * x, axis=1, keepdims=True)
    )


def input_grad(x, dm, grads, gains, groups):
    tokens, width = x.shape
    block = pl.BlockSpec((TBLOCK, width), lambda i: (i, 0))
    return pl.pallas_call(
        functools.partial(input_grad_kernel, [place for _, *place in groups], width),
        name="input_grad",
        out_shape=jax.ShapeDtypeStruct((tokens, width), F32),
        grid=(tokens // TBLOCK,),
        in_specs=[block, block, pl.BlockSpec((TBLOCK, 3 * width), lambda i: (i, 0)), whole((8, width))]
        + [ANY] * len(groups),
        out_specs=block,
        scratch_shapes=[
            pltpu.VMEM((width, columns_of(groups)), BF),
            pltpu.SemaphoreType.DMA,
        ],
        cost_estimate=cost(6 * tokens * width * width, 6 * width * width + 16 * tokens * width),
    )(x, dm, grads, gains, *[piece for piece, *_ in groups])


def flip(values, bits):
    count = lax.axis_size("fsdp")
    return lax.ppermute(values, "fsdp", [(i, i ^ bits) for i in range(count)])


def across(values):
    return lax.ppermute(values, "seq", [(0, 1), (1, 0)])


def aligned(rows, down_rows, width, hidden_width, count):
    rest = 2 * hidden_width % width
    return (
        count == 16
        and rows % 16 == 0
        and down_rows % 16 == 0
        and (rest == 0 or (width % rest == 0 and rows * rest % (16 * width) == 0))
    )


def gate(values, *others):
    return lax.optimization_barrier((values,) + others)[0]


def gather_rows(shard, parts, before):
    if parts == 1:
        return [(lax.all_gather(shard, "fsdp", axis=0, tiled=True), (0,), 0)]
    uppers = tuple(range(0, parts, 4))
    mine = jnp.concatenate([shard] + [flip(shard, upper) for upper in uppers[1:]])
    beside = flip(mine, 2)
    got = [(mine, 0, 0), (beside, 2, 0), (across(gate(mine, before)), 0, 1), (across(beside), 2, 1)]
    got += [(flip(piece, 1), low + 1, side) for piece, low, side in got]
    return [(piece, tuple(upper + low for upper in uppers), side) for piece, low, side in got]


def pack_kernel(q_ref, k_ref, v_ref, column_ref, out_ref, gate_ref, up_ref, down_ref, in_ref, packed_ref):
    rows, width = out_ref.shape
    hidden_width = gate_ref.shape[1]
    half = in_ref.shape[1]
    for rank in range(2):

        @pl.when(lax.axis_index("seq") == rank)
        def _(rank=rank):
            left = 0
            for piece in (q_ref, k_ref, v_ref, column_ref):
                start, stop = max(left, rank * half), min(left + piece.shape[1], (rank + 1) * half)
                if start < stop:
                    in_ref[:, start - rank * half : stop - rank * half] = piece[:, start - left : stop - left]
                left += piece.shape[1]

    slices, _ = packed_slices(rows, down_ref.shape[0], width, hidden_width)
    for name, (low, high), (left, right), top, column in slices:
        spans = {
            "down": [(down_ref, left, right, 0)],
            "out": [(out_ref, left, right, 0)],
            "both": [
                (gate_ref, left, min(right, hidden_width), 0),
                (up_ref, max(left, hidden_width), right, hidden_width),
            ],
        }[name]
        for array, start, stop, base in spans:
            if start < stop:
                packed_ref[top : top + high - low, column + start - left : column + stop - left] = array[
                    low:high, start - base : stop - base
                ]


def pack(w_query, w_key, w_value, column, w_out, w_gate, w_up, w_down):
    rows, width = w_out.shape
    _, height = packed_slices(rows, w_down.shape[0], width, w_gate.shape[1])
    given = (w_query, w_key, w_value, column, w_out, w_gate, w_up, w_down)
    return pl.pallas_call(
        pack_kernel,
        name="pack",
        out_shape=[
            jax.ShapeDtypeStruct((rows, (3 * width + column.shape[1]) // 2), BF),
            jax.ShapeDtypeStruct((height, width), BF),
        ],
    )(*given)


class Scatter:
    def __init__(self, outs, parts, rank):
        self.parts, self.rank = parts, rank
        if parts == 1:
            self.total = lax.psum_scatter(outs[0], "fsdp", scatter_dimension=0, tiled=True)
            return
        self.keep, send = outs
        self.got = flip(send, 1)
        self.half = self.keep.shape[2] // 2

    def columns(self, side, rows):
        at = lax.bitwise_xor(self.rank, side) * self.half
        kept, got = [lax.dynamic_slice_in_dim(array, at, self.half, 2)[rows] for array in (self.keep, self.got)]
        return kept.astype(F32) + got.astype(F32)

    def x_hop(self):
        if self.parts == 1:
            return []
        aside = self.columns(1, slice(None)).astype(BF)
        self.aside = across(aside)
        return [aside]

    def y_hop(self):
        if self.parts == 1:
            return []
        upper = slice(self.parts // 4, None)
        ahead = (self.columns(0, upper) + self.aside[upper].astype(F32)).astype(BF)
        self.ahead = flip(ahead, 2)
        return [ahead]

    def z_hop(self):
        if self.parts == 1:
            return []
        lower = slice(0, self.parts // 4)
        sums = self.columns(0, lower) + self.aside[lower].astype(F32) + self.ahead.astype(F32)
        self.own, sends = sums[0], [total.astype(BF) for total in sums[1:]]
        self.others = [flip(send, 4 * (j + 1)) for j, send in enumerate(sends)]
        return sends

    def result(self):
        if self.parts == 1:
            return self.total.astype(F32) + across(self.total).astype(F32)
        total = self.own
        for piece in self.others:
            total = total + piece.astype(F32)
        total = total.astype(BF)
        partner = across(total)
        first = jnp.where(self.rank == 0, total, partner)
        second = jnp.where(self.rank == 0, partner, total)
        return jnp.concatenate([first, second], axis=1).astype(F32)


def rope_tables(length):
    half = HEAD_DIM // 2
    inverse = jnp.exp(jnp.arange(half, dtype=F32) * (-2.0 * math.log(10000.0) / HEAD_DIM))
    low = jnp.arange(32, dtype=jnp.int32).astype(F32)[:, None] * inverse[None, :]
    high = (jnp.arange(length // 32, dtype=jnp.int32) * 32).astype(F32)[:, None] * inverse[None, :]
    cos_low, sin_low = jnp.cos(low)[None], jnp.sin(low)[None]
    cos_high, sin_high = jnp.cos(high)[:, None], jnp.sin(high)[:, None]
    cosine = (cos_high * cos_low - sin_high * sin_low).reshape(length, half)
    sine = (sin_high * cos_low + cos_high * sin_low).reshape(length, half)
    return (
        jnp.concatenate([cosine] * 4, axis=1),
        jnp.concatenate([-sine, sine, -sine, sine], axis=1),
    )


def per_device(
    tokens, doc_ids, cotangent, w_query, w_key, w_value, w_out, w_gate, w_up, w_down, gain_attn, gain_ffn
):
    seq_rank = lax.axis_index("seq")
    count = lax.axis_size("fsdp")
    micro, _, span, width = tokens.shape
    hidden_width = w_gate.shape[1]
    rows = w_query.shape[0]
    parts = count if aligned(rows, w_down.shape[0], width, hidden_width, count) else 1

    column = jnp.pad(jnp.stack([gain_attn, gain_ffn], axis=1), ((0, 0), (0, 254)))
    if parts == 1:
        w_in = jnp.concatenate([w_query, w_key, w_value, column], axis=1)
        given = [lax.all_gather(weight, "fsdp", axis=0, tiled=True) for weight in (w_out, w_gate, w_up, w_down)]
    else:
        w_in, packed = pack(w_query, w_key, w_value, column, w_out, w_gate, w_up, w_down)
        given = [lax.all_gather(packed, "fsdp", axis=0, tiled=True)]

    def exchanged(array):
        own = lax.dynamic_index_in_dim(array, seq_rank, 0, keepdims=False)[0]
        return own, lax.dynamic_index_in_dim(array, 1 - seq_rank, 0, keepdims=False)[0]

    def ordered(own, other):
        return jnp.where(seq_rank == 0, jnp.concatenate([own, other]), jnp.concatenate([other, own]))

    def halves(array):
        own = lax.dynamic_slice_in_dim(array, seq_rank * span, span, 0)
        other = lax.dynamic_slice_in_dim(array, (1 - seq_rank) * span, span, 0)
        return own, other

    def give_back(own, other):
        first, second = jnp.where(seq_rank == 0, own, other), jnp.where(seq_rank == 0, other, own)
        return jnp.stack([first, second])[:, None]

    own_x, other_x = exchanged(tokens)
    other_x = across(other_x)
    groups_in = gather_rows(w_in, parts, other_x)
    x = ordered(own_x, other_x)
    own_docs, other_docs = exchanged(doc_ids)
    docs = ordered(own_docs, across(other_docs))
    own_dy, other_dy = exchanged(gate(cotangent, x, *[piece for piece, *_ in groups_in]))
    dy = ordered(own_dy, across(other_dy))

    length = x.shape[0]
    cosine, sine = rope_tables(length)
    starts = jnp.sum((docs[None, :] < docs[:, None]).astype(jnp.int32), axis=1)
    first = starts[::QBLOCK] // QBLOCK
    starts = starts[None, :]

    normed, queries, keys, values, gains = project(x, cosine, sine, groups_in)
    attended, lse = attend(queries, keys, values, starts, first)
    y, normed_two, hidden, dgate, dup, dm, dmr, datt = feed(
        x, attended, dy, gains, given, rows if parts > 1 else width, hidden_width
    )
    own_y, other_y = halves(y)
    other_y = across(other_y)
    output = give_back(own_y, other_y)

    if parts == 1:
        sum_gate, sum_up, sum_down = [
            lax.psum_scatter(outer_sums(1, [(lefts, right)], tile, name)[0], "fsdp", scatter_dimension=0, tiled=True)
            for lefts, right, tile, name in (
                ([normed_two], dgate, 512, "grad_gate"),
                ([normed_two], dup, 512, "grad_up"),
                ([hidden], dy, width // 2, "grad_down"),
            )
        ]
        sums = (sum_gate, sum_up, sum_down)
    else:
        ff = feed_grads(parts, normed_two, dgate, dup, hidden, dy)
        datt = gate(datt, ff)
        ff = lax.psum_scatter(ff.reshape(-1, hidden_width), "fsdp", scatter_dimension=0, tiled=True)
        sums = (ff,)
    grads = attend_back(queries, keys, values, datt, lse, starts, first, cosine, sine)
    scatter = Scatter(
        outer_sums(parts, [([gate(normed, grads, other_y)], grads), ([attended], dmr)], width, "grad_in"), parts, seq_rank
    )
    sent = scatter.x_hop()
    grad_x = input_grad(gate(x, *sent), dm, grads, gains, groups_in)
    own_g, other_g = halves(grad_x)
    other_g = other_g.astype(BF)
    if parts > 1:
        scatter.aside = gate(scatter.aside, other_g)
    sent = scatter.y_hop()
    other_g = across(gate(other_g, *sent))
    sent = scatter.z_hop()
    sums = [part.astype(F32) + across(gate(part, *sent)).astype(F32) for part in sums]
    grad_tokens = give_back(own_g, gate(other_g, *sent).astype(F32))
    sum_in = scatter.result()
    if parts == 1:
        sum_gate, sum_up, sum_down = sums
    else:
        sum_gate, sum_up, rest = sums[0][:rows], sums[0][rows : 2 * rows], sums[0][2 * rows :]
        unit = 16 * parts
        rest = rest.reshape(rows // 16, 16, hidden_width // unit, unit)
        sum_down = rest.transpose(2, 1, 0, 3).reshape(w_down.shape)

    sum_in, sum_out = sum_in[:, : 3 * width], sum_in[:, 3 * width :]
    grad_gain_attn = sum(
        jnp.sum(weight.astype(F32) * sum_in[:, at * width : (at + 1) * width], axis=1)
        for at, weight in enumerate((w_query, w_key, w_value))
    ) / gain_attn.astype(F32)
    grad_gain_ffn = (
        jnp.sum(w_gate.astype(F32) * sum_gate, axis=1) + jnp.sum(w_up.astype(F32) * sum_up, axis=1)
    ) / gain_ffn.astype(F32)
    by_part = [sum_in[:, at * width : (at + 1) * width] for at in range(3)]
    return (output, grad_tokens, *by_part, sum_out, sum_gate, sum_up, sum_down, grad_gain_attn, grad_gain_ffn)


def solution(mesh):
    rows = P("fsdp", None)
    acts = P(None, "fsdp", "seq", None)
    return jax.shard_map(
        per_device,
        mesh=mesh,
        in_specs=(acts, P(None, "fsdp", "seq"), acts) + (rows,) * 7 + (P("fsdp"),) * 2,
        out_specs=(acts, acts) + (rows,) * 7 + (P("fsdp"),) * 2,
        check_vma=False,
    )
```

```python
import functools
import math

import jax
import jax.numpy as jnp
from jax import lax
from jax.experimental import pallas as pl
from jax.experimental.pallas import tpu as pltpu
from jax.sharding import PartitionSpec as P

HEAD_DIM = 64
EPSILON = 1e-05
MASK_FILL = -1e30
LONGEST = 512
PAIR = 2 * HEAD_DIM
QBLOCK = 128
TBLOCK = 512
FBLOCK = 512
FSTEP = 512
TILE = 1024
BF = jnp.bfloat16
F32 = jnp.float32
ANY = pl.BlockSpec(memory_space=pl.ANY)


def cost(flops, nbytes, trans=0):
    return pl.CostEstimate(flops=int(flops), bytes_accessed=int(nbytes), transcendentals=int(trans))


def whole(shape):
    zeros = (0,) * len(shape)
    return pl.BlockSpec(shape, lambda *_: zeros)


def dot_nt(left, right):
    return lax.dot_general(left, right, (((1,), (1,)), ((), ())), preferred_element_type=F32)


def dot_nn(left, right):
    return lax.dot_general(left, right, (((1,), (0,)), ((), ())), preferred_element_type=F32)


def swap_halves(values):
    lane = lax.broadcasted_iota(jnp.int32, values.shape, 1)
    width = values.shape[1]
    half = HEAD_DIM // 2
    ahead = pltpu.roll(values, width - half, 1)
    behind = pltpu.roll(values, half, 1)
    return jnp.where((lane & (HEAD_DIM - 1)) < half, ahead, behind)


def wide(table, width):
    return jnp.concatenate([table] * (width // table.shape[1]), axis=1)


def load_copies(groups, scratch, sem):
    if len(groups) == 1:
        return [pltpu.make_async_copy(groups[0][0], scratch, sem)]
    me, rank = lax.axis_index("fsdp"), lax.axis_index("seq")
    rows = 2 * scratch.shape[0] // sum(len(places) for _, places, _ in groups)
    half = scratch.shape[1] // 2
    copies = []
    for piece, places, side in groups:
        columns = pl.ds(pl.multiple_of(lax.bitwise_xor(rank, side) * half, 128), half)
        for at, place in enumerate(places):
            target = pl.ds(pl.multiple_of(lax.bitwise_xor(me, place) * rows, 16), rows)
            copies.append(
                pltpu.make_async_copy(piece.at[pl.ds(at * rows, rows), :], scratch.at[target, columns], sem)
            )
    return copies


def columns_of(groups):
    return groups[0][0].shape[1] * (1 if len(groups) == 1 else 2)


def start_all(copies):
    for copy in copies:
        copy.start()


def wait_all(copies):
    for copy in copies:
        copy.wait()


def rows_of(block):
    return jnp.transpose(block.astype(F32))[0:8, :]


def project_kernel(places, width, *refs):
    x_ref, cos_ref, sin_ref = refs[:3]
    count = len(places)
    groups = [(piece, *place) for piece, place in zip(refs[3 : 3 + count], places)]
    n_ref, q_ref, k_ref, v_ref, gains_ref = refs[3 + count : 8 + count]
    weights, gain, sem = refs[8 + count :]

    @pl.when(pl.program_id(0) == 0)
    def _():
        copies = load_copies(groups, weights, sem)
        start_all(copies)
        wait_all(copies)
        gain[...] = rows_of(weights[:, 3 * width : 3 * width + 128])
        gains_ref[...] = gain[...]

    x = x_ref[...].astype(F32)
    inverse = lax.rsqrt(jnp.mean(x * x, axis=1, keepdims=True) + EPSILON)
    normed = (x * inverse * gain[0:1, :]).astype(BF)
    n_ref[...] = normed
    cosine, sine = wide(cos_ref[...], width // 2), wide(sin_ref[...], width // 2)
    for part, out in enumerate((q_ref, k_ref)):
        for at in range(0, width, width // 2):
            linear = dot_nn(normed, weights[:, part * width + at : part * width + at + width // 2])
            turned = (linear * cosine + swap_halves(linear) * sine).astype(BF)
            if part == 0:
                turned = turned * jnp.asarray(HEAD_DIM**-0.5, BF)
            out[:, at : at + width // 2] = turned
    v_ref[...] = dot_nn(normed, weights[:, 2 * width : 3 * width]).astype(BF)


def project(x, cosine, sine, groups):
    tokens, width = x.shape
    total = columns_of(groups)
    shape = jax.ShapeDtypeStruct((tokens, width), BF)
    block = pl.BlockSpec((TBLOCK, width), lambda i: (i, 0))
    table = pl.BlockSpec((TBLOCK, PAIR), lambda i: (i, 0))
    return pl.pallas_call(
        functools.partial(project_kernel, [place for _, *place in groups], width),
        name="project",
        out_shape=[shape] * 4 + [jax.ShapeDtypeStruct((8, width), F32)],
        grid=(tokens // TBLOCK,),
        in_specs=[block, table, table] + [ANY] * len(groups),
        out_specs=[block] * 4 + [whole((8, width))],
        scratch_shapes=[
            pltpu.VMEM((width, total), BF),
            pltpu.VMEM((8, width), F32),
            pltpu.SemaphoreType.DMA,
        ],
        cost_estimate=cost(6 * tokens * width * width, 6 * width * width + 10 * tokens * width),
    )(x, cosine, sine, *[piece for piece, *_ in groups])


def split_heads(values):
    lane = lax.broadcasted_iota(jnp.int32, values.shape, 1)
    zero = jnp.zeros_like(values)
    return jnp.concatenate(
        [jnp.where(lane < HEAD_DIM, values, zero), jnp.where(lane < HEAD_DIM, zero, values)], axis=0
    )


def join_heads(both):
    rows = both.shape[1] // 2
    own = jnp.concatenate([both[:HEAD_DIM, :rows], both[HEAD_DIM:, rows:]], axis=0)
    return jnp.transpose(own)


def masked_bias(starts_row, first_key, span, first_row):
    key = first_key + lax.broadcasted_iota(jnp.int32, (span, QBLOCK), 0)
    query = first_row + lax.broadcasted_iota(jnp.int32, (span, QBLOCK), 1)
    allowed = (key >= starts_row) & (key <= query)
    return jnp.where(allowed, 0.0, MASK_FILL)


def per_span(first_ref, length, body):
    block = pl.program_id(0)
    seen = block - first_ref[block] + 1
    most = min(length, LONGEST + QBLOCK) // QBLOCK
    for blocks in range(1, most + 1):

        @pl.when(seen == blocks)
        def _(blocks=blocks):
            first_key = pl.multiple_of((block - blocks + 1) * QBLOCK, QBLOCK)
            body(blocks * QBLOCK, first_key, block * QBLOCK)


def attend_kernel(pairs, first_ref, q_ref, k_ref, v_ref, starts_ref, out_ref, lse_ref, v_turned, bias):
    @pl.when(pl.program_id(0) == 0)
    def _():
        v_turned[...] = jnp.transpose(v_ref[...])

    def body(span, first_key, first_row):
        bias[:span, :] = masked_bias(starts_ref[...], first_key, span, first_row)
        keys_at = pl.ds(first_key, span)
        lanes = [slice(pair * PAIR, (pair + 1) * PAIR) for pair in range(pairs)]
        scored, weighed = {}, {}
        for step in range(pairs + 2):
            if step < pairs:
                scored[step] = dot_nt(k_ref[keys_at, lanes[step]], split_heads(q_ref[:, lanes[step]])).astype(BF)
            pair = step - 2
            if pair >= 0:
                weights, total = weighed.pop(pair)
                both = dot_nn(v_turned[lanes[pair], keys_at], weights) * (1.0 / total)
                out_ref[:, lanes[pair]] = join_heads(both).astype(BF)
            pair = step - 1
            if 0 <= pair < pairs:
                fill = bias[:span, :]
                scores = scored.pop(pair).astype(F32) + jnp.concatenate([fill, fill], axis=1)
                top = jnp.max(scores, axis=0, keepdims=True)
                weights = jnp.exp(scores - top)
                total = jnp.sum(weights, axis=0, keepdims=True)
                lse_ref[0, pair : pair + 1, :] = top + jnp.log(total)
                weighed[pair] = (weights.astype(BF), total)

    per_span(first_ref, k_ref.shape[0], body)


def attend(queries, keys, values, starts, first):
    length, width = queries.shape
    pairs = width // PAIR
    blocks = length // QBLOCK
    block = pl.BlockSpec((QBLOCK, width), lambda i, f: (i, 0))
    return pl.pallas_call(
        functools.partial(attend_kernel, pairs),
        name="attend",
        out_shape=[
            jax.ShapeDtypeStruct((length, width), BF),
            jax.ShapeDtypeStruct((blocks, pairs, 2 * QBLOCK), F32),
        ],
        grid_spec=pltpu.PrefetchScalarGridSpec(
            num_scalar_prefetch=1,
            grid=(blocks,),
            in_specs=[
                block,
                whole((length, width)),
                whole((length, width)),
                pl.BlockSpec((1, QBLOCK), lambda i, f: (0, i)),
            ],
            out_specs=[block, pl.BlockSpec((1, pairs, 2 * QBLOCK), lambda i, f: (i, 0, 0))],
            scratch_shapes=[
                pltpu.VMEM((width, length), BF),
                pltpu.VMEM((min(length, LONGEST + QBLOCK), QBLOCK), F32),
            ],
        ),
        cost_estimate=cost(4 * length * length * width, 10 * length * width),
    )(first, queries, keys, values, starts)


def attend_back_kernel(
    pairs, first_ref, q_ref, k_ref, v_ref, g_ref, lse_ref, starts_ref, cos_ref, sin_ref, out_ref, k_turned, bias, dk, dv
):
    width = pairs * PAIR
    block = pl.program_id(0)

    @pl.when(block == 0)
    def _():
        k_turned[...] = jnp.transpose(k_ref[...])
        dk[...] = jnp.zeros_like(dk)
        dv[...] = jnp.zeros_like(dv)

    rows = pl.ds(pl.multiple_of(block * QBLOCK, QBLOCK), QBLOCK)
    cosine, sine = cos_ref[rows, :], sin_ref[rows, :]

    def body(span, first_key, first_row):
        bias[:span, :] = masked_bias(starts_ref[...], first_key, span, first_row)
        keys_at = pl.ds(first_key, span)
        lanes = [slice(pair * PAIR, (pair + 1) * PAIR) for pair in range(pairs)]
        scored, ready = {}, {}
        for step in range(pairs + 2):
            if step < pairs:
                at = lanes[step]
                queries, grads = split_heads(q_ref[:, at]), split_heads(g_ref[:, at])
                scores = dot_nt(k_ref[keys_at, at], queries).astype(BF)
                scored[step] = (scores, dot_nt(v_ref[keys_at, at], grads), queries, grads)
            pair = step - 2
            if pair >= 0:
                at = lanes[pair]
                probs, grad_scores, queries, grads = ready.pop(pair)
                dv[keys_at, at] += dot_nn(probs, grads)
                dk[keys_at, at] += dot_nn(grad_scores, queries)
                both = dot_nn(k_turned[at, keys_at], grad_scores)
                dq = (join_heads(both) * HEAD_DIM**-0.5).astype(BF).astype(F32)
                out_ref[rows, at] = (dq * cosine - swap_halves(dq) * sine).astype(BF)
            pair = step - 1
            if 0 <= pair < pairs:
                scores, grad_probs, queries, grads = scored.pop(pair)
                fill = bias[:span, :]
                scores = scores.astype(F32) + jnp.concatenate([fill, fill], axis=1)
                probs = jnp.exp(scores - lse_ref[0, pair : pair + 1, :])
                delta = jnp.sum(probs * grad_probs, axis=0, keepdims=True)
                ready[pair] = (probs.astype(BF), (probs * (grad_probs - delta)).astype(BF), queries, grads)

    per_span(first_ref, k_ref.shape[0], body)

    @pl.when(block == pl.num_programs(0) - 1)
    def _():
        def finish(step, carry):
            at = pl.ds(pl.multiple_of(step * QBLOCK, QBLOCK), QBLOCK)
            turn, slant = cos_ref[at, :], sin_ref[at, :]
            for pair in range(pairs):
                lanes = slice(pair * PAIR, (pair + 1) * PAIR)
                grad = dk[at, lanes].astype(BF).astype(F32)
                out_ref[at, width + pair * PAIR : width + (pair + 1) * PAIR] = (
                    grad * turn - swap_halves(grad) * slant
                ).astype(BF)
            out_ref[at, 2 * width : 3 * width] = dv[at, :].astype(BF)
            return carry

        lax.fori_loop(0, k_ref.shape[0] // QBLOCK, finish, 0)


def attend_back(queries, keys, values, grads, lse, starts, first, cosine, sine):
    length, width = queries.shape
    pairs = width // PAIR
    blocks = length // QBLOCK
    block = pl.BlockSpec((QBLOCK, width), lambda i, f: (i, 0))
    full = whole((length, width))
    table = whole((length, PAIR))
    return pl.pallas_call(
        functools.partial(attend_back_kernel, pairs),
        name="attend_back",
        out_shape=jax.ShapeDtypeStruct((length, 3 * width), BF),
        grid_spec=pltpu.PrefetchScalarGridSpec(
            num_scalar_prefetch=1,
            grid=(blocks,),
            in_specs=[
                block,
                full,
                full,
                block,
                pl.BlockSpec((1, pairs, 2 * QBLOCK), lambda i, f: (i, 0, 0)),
                pl.BlockSpec((1, QBLOCK), lambda i, f: (0, i)),
                table,
                table,
            ],
            out_specs=whole((length, 3 * width)),
            scratch_shapes=[
                pltpu.VMEM((width, length), BF),
                pltpu.VMEM((min(length, LONGEST + QBLOCK), QBLOCK), F32),
                pltpu.VMEM((length, width), F32),
                pltpu.VMEM((length, width), F32),
            ],
        ),
        cost_estimate=cost(10 * length * length * width, 16 * length * width),
    )(first, queries, keys, values, grads, lse, starts, cosine, sine)


def packed_slices(rows, down_rows, width, hidden_width):
    slices = [("down", (0, down_rows), (0, width), 0, 0), ("out", (0, rows), (0, width), down_rows, 0)]
    top = down_rows + rows
    both = 2 * hidden_width
    for at in range(0, both - width + 1, width):
        slices.append(("both", (0, rows), (at, at + width), top, 0))
        top += rows
    rest = both % width
    if rest:
        few = rows * rest // width
        for place in range(width // rest):
            slices.append(("both", (place * few, (place + 1) * few), (both - rest, both), top, place * rest))
        top += few
    return slices, top


def feed_copies(packed, targets, owner, sems, wanted):
    w_out, w_both, w_down = targets
    parts = w_out.shape[0] // packed[0]
    hidden_width = w_down.shape[0]
    step = min(FSTEP, hidden_width)
    rows, down_rows = packed[0], hidden_width // parts
    slices, height = packed_slices(rows, down_rows, w_out.shape[1], hidden_width)
    kinds = {"out": (w_out, rows), "both": (w_both, rows), "down": (w_down, down_rows)}
    copies = []
    for name, (low, high), (left, right), top, column in slices:
        due = name
        if name == "both":
            crosses = left < hidden_width < right
            due = 0 if crosses else left % hidden_width // step
        if due != wanted:
            continue
        target, each = kinds[name]
        number = due + 2 if name == "both" else ("out", "down").index(name)
        source = packed[1].at[
            pl.ds(pl.multiple_of(owner * height + top, 16), high - low), column : column + right - left
        ]
        goal = target.at[pl.ds(pl.multiple_of(owner * each + low, 16), high - low), left:right]
        copies.append(pltpu.make_async_copy(source, goal, sems.at[number]))
    return copies


def feed_kernel(rows, count, width, hidden_width, *refs):
    x_ref, att_ref, dy_ref, gain_ref = refs[:4]
    given, refs = refs[4 : 4 + count], refs[4 + count :]
    y_ref, n_ref, hid_ref, dgate_ref, dup_ref, dm_ref, dmr_ref, datt_ref = refs[:8]
    w_out, w_both, w_down, result, back, sems = refs[8:]
    targets = (w_out, w_both, w_down)
    parts = width // rows

    def whole_copies():
        views = (w_out, w_both.at[:, :hidden_width], w_both.at[:, hidden_width:], w_down)
        return [pltpu.make_async_copy(piece, view, sems.at[0]) for piece, view in zip(given, views)]

    chunks = hidden_width // min(FSTEP, hidden_width)

    def per_owner(act, wanted):
        def step(owner, carry):
            act(feed_copies((rows, given[0]), targets, owner, sems, wanted))
            return carry

        lax.fori_loop(0, parts, step, 0)

    opening = pl.program_id(0) == 0

    @pl.when(opening)
    def _():
        if count > 1:
            copies = whole_copies()
            start_all(copies)
            wait_all(copies)
        else:
            for wanted in ("out", 0, "down", *range(1, chunks)):
                per_owner(start_all, wanted)

    def wait_for(wanted):
        if count == 1:

            @pl.when(opening)
            def _():
                per_owner(wait_all, wanted)

    wait_for("out")
    gain = gain_ref[1:2, :]
    dy = dy_ref[...]
    middle = x_ref[...].astype(F32) + dot_nn(att_ref[...], w_out[...])
    inverse = lax.rsqrt(jnp.mean(middle * middle, axis=1, keepdims=True) + EPSILON)
    normed = (middle * inverse * gain).astype(BF)
    n_ref[...] = normed
    wait_for("down")
    result[...] = middle
    back[...] = jnp.zeros_like(middle)
    step = min(FSTEP, hidden_width)

    def chunk(number, carry):
        at = pl.multiple_of(number * step, step)
        part = pl.ds(at, step)
        for wanted in range(chunks):

            @pl.when(number == wanted)
            def _(wanted=wanted):
                wait_for(wanted)

        w_gate = w_both[:, part]
        w_up = w_both[:, pl.ds(pl.multiple_of(hidden_width + at, step), step)]
        gate = dot_nn(normed, w_gate)
        up = dot_nn(normed, w_up)
        dh = dot_nt(dy, w_down[part, :])
        sigma = 1.0 / (1.0 + jnp.exp(-gate))
        silu = gate * sigma
        hidden = (silu * up).astype(BF)
        hid_ref[:, part] = hidden
        dgate = (dh * up * (sigma * (1.0 + gate * (1.0 - sigma)))).astype(BF)
        dup = (dh * silu).astype(BF)
        dgate_ref[:, part] = dgate
        dup_ref[:, part] = dup
        result[...] += dot_nn(hidden, w_down[part, :])
        back[...] += dot_nt(dgate, w_gate) + dot_nt(dup, w_up)
        return carry

    lax.fori_loop(0, hidden_width // step, chunk, 0)
    y_ref[...] = result[...].astype(BF)
    scaled = back[...] * gain
    dm = dy.astype(F32) + inverse * scaled - middle * (inverse * inverse * inverse) * jnp.mean(
        scaled * middle, axis=1, keepdims=True
    )
    dm_ref[...] = dm
    dmr = dm.astype(BF)
    dmr_ref[...] = dmr
    datt_ref[...] = dot_nt(dmr, w_out[...]).astype(BF)


def feed(x, attended, dy, gain, given, rows, hidden_width):
    tokens, width = x.shape
    block = pl.BlockSpec((FBLOCK, width), lambda i: (i, 0))
    broad = pl.BlockSpec((FBLOCK, hidden_width), lambda i: (i, 0))
    narrow, large = jax.ShapeDtypeStruct((tokens, width), BF), jax.ShapeDtypeStruct((tokens, hidden_width), BF)
    return pl.pallas_call(
        functools.partial(feed_kernel, rows, len(given), width, hidden_width),
        name="feed",
        out_shape=[narrow, narrow, large, large, large, jax.ShapeDtypeStruct((tokens, width), F32), narrow, narrow],
        grid=(tokens // FBLOCK,),
        in_specs=[block, block, block, whole((8, width))] + [ANY] * len(given),
        out_specs=[block, block, broad, broad, broad, block, block, block],
        scratch_shapes=[
            pltpu.VMEM((width, width), BF),
            pltpu.VMEM((width, 2 * hidden_width), BF),
            pltpu.VMEM((hidden_width, width), BF),
            pltpu.VMEM((FBLOCK, width), F32),
            pltpu.VMEM((FBLOCK, width), F32),
            pltpu.SemaphoreType.DMA((2 + hidden_width // min(FSTEP, hidden_width),)),
        ],
        cost_estimate=cost(4 * tokens * width * (width + 3 * hidden_width), 20 * tokens * width + 6 * tokens * hidden_width),
    )(x, attended, dy, gain, *given)


def dot_tn(left, right):
    return lax.dot_general(left, right, (((0,), (0,)), ((), ())), preferred_element_type=F32)


def write_pieces(parts, total, keep, send):
    if parts == 1:
        keep[...] = total[...].astype(BF)
        return
    rows = total.shape[0] // parts
    me = lax.axis_index("fsdp")
    for place in range(parts // 2):
        upper, y_bit = place % (parts // 4), place // (parts // 4)
        for core, out in enumerate((keep, send)):
            owner = lax.bitwise_xor(me, upper * 4 + y_bit * 2 + core)
            out[place] = total[pl.ds(pl.multiple_of(owner * rows, 16), rows), :].astype(BF)


def outer_kernel(parts, counts, edges, *refs):
    lefts = []
    for count in counts:
        lefts.append(refs[:count])
        refs = refs[count:]
    rights, outs, total = refs[: len(counts)], refs[len(counts) : -1], refs[-1]
    step = pl.program_id(0)
    low = 0
    for group, right, high in zip(lefts, rights, edges):

        @pl.when((step >= low) & (step < high))
        def _(group=group, right=right):
            row = 0
            for left in group:
                total[row : row + left.shape[1], :] = dot_tn(left[...], right[...])
                row += left.shape[1]

        low = high
    write_pieces(parts, total, *((outs + (None,))[:2]))


def outer_sums(parts, pairs, tile, name):
    edges, specs, low = [], [], 0
    for lefts, right in pairs:
        steps = right.shape[1] // tile
        specs.append(
            pl.BlockSpec(
                (right.shape[0], tile), lambda j, low=low, steps=steps: (0, jnp.clip(j - low, 0, steps - 1))
            )
        )
        low += steps
        edges.append(low)
    width = low * tile
    tokens = pairs[0][1].shape[0]
    rows = sum(left.shape[1] for left in pairs[0][0])
    every_left = [left for lefts, _ in pairs for left in lefts]
    shape = (rows, width) if parts == 1 else (parts // 2, rows // parts, width)
    out_block = (rows, tile) if parts == 1 else (parts // 2, rows // parts, tile)
    index = (lambda j: (0, j)) if parts == 1 else (lambda j: (0, 0, j))
    n_out = 1 if parts == 1 else 2
    return pl.pallas_call(
        functools.partial(outer_kernel, parts, tuple(len(lefts) for lefts, _ in pairs), tuple(edges)),
        name=name,
        out_shape=[jax.ShapeDtypeStruct(shape, BF)] * n_out,
        grid=(low,),
        in_specs=[whole(left.shape) for left in every_left] + specs,
        out_specs=[pl.BlockSpec(out_block, index)] * n_out,
        scratch_shapes=[pltpu.VMEM((rows, tile), F32)],
        cost_estimate=cost(2 * tokens * rows * width, 2 * tokens * (rows + width) + 2 * rows * width),
    )(*every_left, *[right for _, right in pairs])


def feed_grads_kernel(parts, steps, n_ref, dgate_ref, dup_ref, hid_any, dy_any, out_ref, hidden, dy, total, sems):
    step = pl.program_id(0)
    tile = out_ref.shape[2]
    width = n_ref.shape[1]
    copies = [pltpu.make_async_copy(hid_any, hidden, sems.at[0]), pltpu.make_async_copy(dy_any, dy, sems.at[1])]

    @pl.when(step == 0)
    def _():
        start_all(copies)

    for low, right in ((0, dgate_ref), (steps, dup_ref)):

        @pl.when((step >= low) & (step < low + steps))
        def _(right=right):
            out_ref[...] = dot_tn(n_ref[...], right[...]).astype(BF).reshape(out_ref.shape)

    @pl.when(step == 2 * steps)
    def _():
        wait_all(copies)
        each = hidden.shape[1] // 2
        for at in (0, each):
            grad = dot_tn(hidden[:, at : at + each], dy[...]).astype(BF)
            total[at * parts // hidden.shape[1] : (at + each) * parts // hidden.shape[1]] = grad.reshape(
                parts // 2, hidden.shape[1] // parts, width
            )

    for place in range(steps):

        @pl.when(step == 2 * steps + place)
        def _(place=place):
            unit = 16 * parts
            for group in range(tile // unit):
                rows = slice((place * tile // unit + group) * 16, (place * tile // unit + group + 1) * 16)
                for column in range(width // unit):
                    out_ref[:, column * 16 : (column + 1) * 16, group * unit : (group + 1) * unit] = total[
                        :, rows, column * unit : (column + 1) * unit
                    ]


def feed_grads(parts, normed, dgate, dup, hidden, dy):
    tokens, width = normed.shape
    hidden_width = hidden.shape[1]
    tile = min(TILE, hidden_width)
    steps = hidden_width // tile
    rows = width // parts
    return pl.pallas_call(
        functools.partial(feed_grads_kernel, parts, steps),
        name="feed_grads",
        out_shape=jax.ShapeDtypeStruct((parts, 3 * rows, hidden_width), BF),
        grid=(3 * steps,),
        in_specs=[
            whole((tokens, width)),
            pl.BlockSpec((tokens, tile), lambda j: (0, jnp.minimum(j, steps - 1))),
            pl.BlockSpec((tokens, tile), lambda j: (0, jnp.clip(j - steps, 0, steps - 1))),
            ANY,
            ANY,
        ],
        out_specs=pl.BlockSpec((parts, rows, tile), lambda j: (0, j // steps, j % steps)),
        scratch_shapes=[
            pltpu.VMEM((tokens, hidden_width), BF),
            pltpu.VMEM((tokens, width), BF),
            pltpu.VMEM((parts, hidden_width // parts, width), BF),
            pltpu.SemaphoreType.DMA((2,)),
        ],
        cost_estimate=cost(6 * tokens * width * hidden_width, 6 * tokens * (hidden_width + width)),
    )(normed, dgate, dup, hidden, dy)


def input_grad_kernel(places, width, *refs):
    count = len(places)
    x_ref, dm_ref, grads_ref, gains_ref = refs[:4]
    groups = [(piece, *place) for piece, place in zip(refs[4 : 4 + count], places)]
    out_ref, weights, sem = refs[4 + count :]

    @pl.when(pl.program_id(0) == 0)
    def _():
        copies = load_copies(groups, weights, sem)
        start_all(copies)
        wait_all(copies)

    x = x_ref[...].astype(F32)
    inverse = lax.rsqrt(jnp.mean(x * x, axis=1, keepdims=True) + EPSILON)
    scaled = dot_nt(grads_ref[...], weights[:, : 3 * width]) * gains_ref[0:1, :]
    out_ref[...] = (
        dm_ref[...]
        + inverse * scaled
        - x * (inverse * inverse * inverse) * jnp.mean(scaled * x, axis=1, keepdims=True)
    )


def input_grad(x, dm, grads, gains, groups):
    tokens, width = x.shape
    block = pl.BlockSpec((TBLOCK, width), lambda i: (i, 0))
    return pl.pallas_call(
        functools.partial(input_grad_kernel, [place for _, *place in groups], width),
        name="input_grad",
        out_shape=jax.ShapeDtypeStruct((tokens, width), F32),
        grid=(tokens // TBLOCK,),
        in_specs=[block, block, pl.BlockSpec((TBLOCK, 3 * width), lambda i: (i, 0)), whole((8, width))]
        + [ANY] * len(groups),
        out_specs=block,
        scratch_shapes=[
            pltpu.VMEM((width, columns_of(groups)), BF),
            pltpu.SemaphoreType.DMA,
        ],
        cost_estimate=cost(6 * tokens * width * width, 6 * width * width + 16 * tokens * width),
    )(x, dm, grads, gains, *[piece for piece, *_ in groups])


def flip(values, bits):
    count = lax.axis_size("fsdp")
    return lax.ppermute(values, "fsdp", [(i, i ^ bits) for i in range(count)])


def across(values):
    return lax.ppermute(values, "seq", [(0, 1), (1, 0)])


def aligned(rows, down_rows, width, hidden_width, count):
    rest = 2 * hidden_width % width
    return (
        count == 16
        and rows % 16 == 0
        and down_rows % 16 == 0
        and (rest == 0 or (width % rest == 0 and rows * rest % (16 * width) == 0))
    )


def gate(values, *others):
    return lax.optimization_barrier((values,) + others)[0]


def gather_rows(shard, parts, before):
    if parts == 1:
        return [(lax.all_gather(shard, "fsdp", axis=0, tiled=True), (0,), 0)]
    uppers = tuple(range(0, parts, 4))
    mine = jnp.concatenate([shard] + [flip(shard, upper) for upper in uppers[1:]])
    beside = flip(mine, 2)
    got = [(mine, 0, 0), (beside, 2, 0), (across(gate(mine, before)), 0, 1), (across(beside), 2, 1)]
    got += [(flip(piece, 1), low + 1, side) for piece, low, side in got]
    return [(piece, tuple(upper + low for upper in uppers), side) for piece, low, side in got]


def pack_kernel(q_ref, k_ref, v_ref, column_ref, out_ref, gate_ref, up_ref, down_ref, in_ref, packed_ref):
    rows, width = out_ref.shape
    hidden_width = gate_ref.shape[1]
    half = in_ref.shape[1]
    for rank in range(2):

        @pl.when(lax.axis_index("seq") == rank)
        def _(rank=rank):
            left = 0
            for piece in (q_ref, k_ref, v_ref, column_ref):
                start, stop = max(left, rank * half), min(left + piece.shape[1], (rank + 1) * half)
                if start < stop:
                    in_ref[:, start - rank * half : stop - rank * half] = piece[:, start - left : stop - left]
                left += piece.shape[1]

    slices, _ = packed_slices(rows, down_ref.shape[0], width, hidden_width)
    for name, (low, high), (left, right), top, column in slices:
        spans = {
            "down": [(down_ref, left, right, 0)],
            "out": [(out_ref, left, right, 0)],
            "both": [
                (gate_ref, left, min(right, hidden_width), 0),
                (up_ref, max(left, hidden_width), right, hidden_width),
            ],
        }[name]
        for array, start, stop, base in spans:
            if start < stop:
                packed_ref[top : top + high - low, column + start - left : column + stop - left] = array[
                    low:high, start - base : stop - base
                ]


def pack(w_query, w_key, w_value, column, w_out, w_gate, w_up, w_down):
    rows, width = w_out.shape
    _, height = packed_slices(rows, w_down.shape[0], width, w_gate.shape[1])
    given = (w_query, w_key, w_value, column, w_out, w_gate, w_up, w_down)
    return pl.pallas_call(
        pack_kernel,
        name="pack",
        out_shape=[
            jax.ShapeDtypeStruct((rows, (3 * width + column.shape[1]) // 2), BF),
            jax.ShapeDtypeStruct((height, width), BF),
        ],
    )(*given)


class Scatter:
    def __init__(self, outs, parts, rank):
        self.parts, self.rank = parts, rank
        if parts == 1:
            self.total = lax.psum_scatter(outs[0], "fsdp", scatter_dimension=0, tiled=True)
            return
        self.keep, send = outs
        self.got = flip(send, 1)
        self.half = self.keep.shape[2] // 2

    def columns(self, side, rows):
        at = lax.bitwise_xor(self.rank, side) * self.half
        kept, got = [lax.dynamic_slice_in_dim(array, at, self.half, 2)[rows] for array in (self.keep, self.got)]
        return kept.astype(F32) + got.astype(F32)

    def x_hop(self):
        if self.parts == 1:
            return []
        aside = self.columns(1, slice(None)).astype(BF)
        self.aside = across(aside)
        return [aside]

    def y_hop(self):
        if self.parts == 1:
            return []
        upper = slice(self.parts // 4, None)
        ahead = (self.columns(0, upper) + self.aside[upper].astype(F32)).astype(BF)
        self.ahead = flip(ahead, 2)
        return [ahead]

    def z_hop(self):
        if self.parts == 1:
            return []
        lower = slice(0, self.parts // 4)
        sums = self.columns(0, lower) + self.aside[lower].astype(F32) + self.ahead.astype(F32)
        self.own, sends = sums[0], [total.astype(BF) for total in sums[1:]]
        self.others = [flip(send, 4 * (j + 1)) for j, send in enumerate(sends)]
        return sends

    def result(self):
        if self.parts == 1:
            return self.total.astype(F32) + across(self.total).astype(F32)
        total = self.own
        for piece in self.others:
            total = total + piece.astype(F32)
        total = total.astype(BF)
        partner = across(total)
        first = jnp.where(self.rank == 0, total, partner)
        second = jnp.where(self.rank == 0, partner, total)
        return jnp.concatenate([first, second], axis=1).astype(F32)


def rope_tables(length):
    half = HEAD_DIM // 2
    inverse = jnp.exp(jnp.arange(half, dtype=F32) * (-2.0 * math.log(10000.0) / HEAD_DIM))
    low = jnp.arange(32, dtype=jnp.int32).astype(F32)[:, None] * inverse[None, :]
    high = (jnp.arange(length // 32, dtype=jnp.int32) * 32).astype(F32)[:, None] * inverse[None, :]
    cos_low, sin_low = jnp.cos(low)[None], jnp.sin(low)[None]
    cos_high, sin_high = jnp.cos(high)[:, None], jnp.sin(high)[:, None]
    cosine = (cos_high * cos_low - sin_high * sin_low).reshape(length, half)
    sine = (sin_high * cos_low + cos_high * sin_low).reshape(length, half)
    return (
        jnp.concatenate([cosine] * 4, axis=1),
        jnp.concatenate([-sine, sine, -sine, sine], axis=1),
    )


def per_device(
    tokens, doc_ids, cotangent, w_query, w_key, w_value, w_out, w_gate, w_up, w_down, gain_attn, gain_ffn
):
    seq_rank = lax.axis_index("seq")
    count = lax.axis_size("fsdp")
    micro, _, span, width = tokens.shape
    hidden_width = w_gate.shape[1]
    rows = w_query.shape[0]
    parts = count if aligned(rows, w_down.shape[0], width, hidden_width, count) else 1

    column = jnp.pad(jnp.stack([gain_attn, gain_ffn], axis=1), ((0, 0), (0, 254)))
    if parts == 1:
        w_in = jnp.concatenate([w_query, w_key, w_value, column], axis=1)
        given = [lax.all_gather(weight, "fsdp", axis=0, tiled=True) for weight in (w_out, w_gate, w_up, w_down)]
    else:
        w_in, packed = pack(w_query, w_key, w_value, column, w_out, w_gate, w_up, w_down)
        given = [lax.all_gather(packed, "fsdp", axis=0, tiled=True)]

    def exchanged(array):
        own = lax.dynamic_index_in_dim(array, seq_rank, 0, keepdims=False)[0]
        return own, lax.dynamic_index_in_dim(array, 1 - seq_rank, 0, keepdims=False)[0]

    def ordered(own, other):
        return jnp.where(seq_rank == 0, jnp.concatenate([own, other]), jnp.concatenate([other, own]))

    def halves(array):
        own = lax.dynamic_slice_in_dim(array, seq_rank * span, span, 0)
        other = lax.dynamic_slice_in_dim(array, (1 - seq_rank) * span, span, 0)
        return own, other

    def give_back(own, other):
        first, second = jnp.where(seq_rank == 0, own, other), jnp.where(seq_rank == 0, other, own)
        return jnp.stack([first, second])[:, None]

    own_x, other_x = exchanged(tokens)
    other_x = across(other_x)
    groups_in = gather_rows(w_in, parts, other_x)
    x = ordered(own_x, other_x)
    own_docs, other_docs = exchanged(doc_ids)
    docs = ordered(own_docs, across(other_docs))
    own_dy, other_dy = exchanged(gate(cotangent, x, *[piece for piece, *_ in groups_in]))
    dy = ordered(own_dy, across(other_dy))

    length = x.shape[0]
    cosine, sine = rope_tables(length)
    starts = jnp.sum((docs[None, :] < docs[:, None]).astype(jnp.int32), axis=1)
    first = starts[::QBLOCK] // QBLOCK
    starts = starts[None, :]

    normed, queries, keys, values, gains = project(x, cosine, sine, groups_in)
    attended, lse = attend(queries, keys, values, starts, first)
    y, normed_two, hidden, dgate, dup, dm, dmr, datt = feed(
        x, attended, dy, gains, given, rows if parts > 1 else width, hidden_width
    )
    own_y, other_y = halves(y)
    other_y = across(other_y)
    output = give_back(own_y, other_y)

    if parts == 1:
        sum_gate, sum_up, sum_down = [
            lax.psum_scatter(outer_sums(1, [(lefts, right)], tile, name)[0], "fsdp", scatter_dimension=0, tiled=True)
            for lefts, right, tile, name in (
                ([normed_two], dgate, 512, "grad_gate"),
                ([normed_two], dup, 512, "grad_up"),
                ([hidden], dy, width // 2, "grad_down"),
            )
        ]
        sums = (sum_gate, sum_up, sum_down)
    else:
        ff = feed_grads(parts, normed_two, dgate, dup, hidden, dy)
        datt = gate(datt, ff)
        ff = lax.psum_scatter(ff.reshape(-1, hidden_width), "fsdp", scatter_dimension=0, tiled=True)
        sums = (ff,)
    grads = attend_back(queries, keys, values, datt, lse, starts, first, cosine, sine)
    scatter = Scatter(
        outer_sums(parts, [([gate(normed, grads, other_y)], grads), ([attended], dmr)], width, "grad_in"), parts, seq_rank
    )
    sent = scatter.x_hop()
    grad_x = input_grad(gate(x, *sent), dm, grads, gains, groups_in)
    own_g, other_g = halves(grad_x)
    other_g = other_g.astype(BF)
    if parts > 1:
        scatter.aside = gate(scatter.aside, other_g)
    sent = scatter.y_hop()
    other_g = across(gate(other_g, *sent))
    sent = scatter.z_hop()
    sums = [part.astype(F32) + across(gate(part, *sent)).astype(F32) for part in sums]
    grad_tokens = give_back(own_g, gate(other_g, *sent).astype(F32))
    sum_in = scatter.result()
    if parts == 1:
        sum_gate, sum_up, sum_down = sums
    else:
        sum_gate, sum_up, rest = sums[0][:rows], sums[0][rows : 2 * rows], sums[0][2 * rows :]
        unit = 16 * parts
        rest = rest.reshape(rows // 16, 16, hidden_width // unit, unit)
        sum_down = rest.transpose(2, 1, 0, 3).reshape(w_down.shape)

    sum_in, sum_out = sum_in[:, : 3 * width], sum_in[:, 3 * width :]
    grad_gain_attn = sum(
        jnp.sum(weight.astype(F32) * sum_in[:, at * width : (at + 1) * width], axis=1)
        for at, weight in enumerate((w_query, w_key, w_value))
    ) / gain_attn.astype(F32)
    grad_gain_ffn = (
        jnp.sum(w_gate.astype(F32) * sum_gate, axis=1) + jnp.sum(w_up.astype(F32) * sum_up, axis=1)
    ) / gain_ffn.astype(F32)
    by_part = [sum_in[:, at * width : (at + 1) * width] for at in range(3)]
    return (output, grad_tokens, *by_part, sum_out, sum_gate, sum_up, sum_down, grad_gain_attn, grad_gain_ffn)


def solution(mesh):
    rows = P("fsdp", None)
    acts = P(None, "fsdp", "seq", None)
    return jax.shard_map(
        per_device,
        mesh=mesh,
        in_specs=(acts, P(None, "fsdp", "seq"), acts) + (rows,) * 7 + (P("fsdp"),) * 2,
        out_specs=(acts, acts) + (rows,) * 7 + (P("fsdp"),) * 2,
        check_vma=False,
    )
```
